128 devices in a mesh: dp: 32 (over z_lo, y, x), mp: 4 (over z_hi, core).
Axes of the slice: x: 4, y: 4, z: 4 (z_hi: 2, z_lo: 2; z = z_hi * 2 + z_lo), core: 2. Of those that a mesh axis runs over, the one named last changes fastest.
Arguments:
- queries: bfloat16 [20480, 4096], P('dp', 'mp'), may hold values from -180 to 180
- keys: bfloat16 [20480, 512], P('dp', 'mp'), may hold values from -6 to 6
- values: bfloat16 [20480, 512], P('dp', 'mp'), may hold values from -6 to 6
- prompt_keys: bfloat16 [128, 512], P(None, 'mp'), may hold values from -6 to 6
- prompt_values: bfloat16 [128, 512], P(None, 'mp'), may hold values from -6 to 6
- out_weight: bfloat16 [4096, 8192], P('mp', 'dp'), may hold values from -0.09375 to 0.09375
- out_grad: bfloat16 [20480, 8192], P('dp'), may hold values from -6 to 6
- lengths: int32 [32, 8], P('dp'), may hold values from 1 to 320, 640 in all within a row
Outputs:
- mixed: bfloat16 [20480, 8192], P('dp', 'mp')
- prompt_key_grad: float32 [128, 512], P('dp', 'mp')
- prompt_value_grad: float32 [128, 512], P('dp', 'mp')
The draws below stay inside these ranges and needn't reach their ends.
All inputs are finite; a program needn't handle non-finite values.
Results may differ from the reference program's by a relative error of at most 0.024.
Values may be sent and summed in bfloat16 or wider, within the bound.
A program may use at most 192 MiB of HBM per device.

```python
import math
import jax
import jax.numpy as jnp
import numpy as np
from jax import lax

D = 8192
HEADS = 32
KV_HEADS = 4
HD = 128
PROMPT = 128
DOCS = 8
TOK_DEV = 640
DOC_MOST = 320
TOKENS = 20480
N_DP = 32
N_MP = 4


def drawn_pair(key):
    keys_f = jnp.clip(jax.random.normal(jax.random.fold_in(key, 11), (TOKENS, KV_HEADS * HD), jnp.float32), -6.0, 6.0)
    query_f = jnp.clip(jax.random.normal(jax.random.fold_in(key, 12), (TOKENS, HEADS * HD), jnp.float32), -6.0, 6.0)
    return (keys_f, query_f)


def draw_queries(key, part):
    return drawn_pair(key)[1].astype(jnp.bfloat16)


def draw_keys(key, part):
    return drawn_pair(key)[0].astype(jnp.bfloat16)


def steps_of(rng, extent, shards, smallest, top_value):
    gain, own = 1.0, jax.random.fold_in(rng, 6)
    for dim, shards_of in shards:
        steps = jnp.exp(jax.random.uniform(jax.random.fold_in(own, dim), (shards_of,), jnp.float32, smallest / len(shards), top_value / len(shards)))
        gain = gain * jnp.repeat(steps, extent[dim] // shards_of).reshape([-1 if axis == dim else 1 for axis in range(len(extent))])
    return gain


def length_profile(number_of, total, bound, skew):
    portions = [(1 << 20) // math.isqrt(rank ** skew) + 1 for rank in range(2, number_of + 1)]
    spare, holding = total - bound - (number_of - 1), [1] * (number_of - 1)
    while spare > 0:
        candidates = [i for i in range(number_of - 1) if holding[i] < bound]
        mass, left = sum([portions[i] for i in candidates]), spare
        for i in candidates:
            addition = min(bound - holding[i], max(1, left * portions[i] // mass), spare)
            holding[i] = holding[i] + addition
            spare = spare - addition
    return np.array([bound] + holding)


def ragged(key, number_of, total, limit, skew):
    if number_of == 2:
        one = jax.random.randint(key, (), max(1, total - limit), min(limit, total - 1) + 1)
        return jnp.stack([one, total - one])
    sizes = jnp.asarray(length_profile(number_of, total, limit, skew), jnp.int32)
    twos = (number_of - 1) // 2
    giver, sink = sizes[1:1 + 2 * twos:2], sizes[2:2 + 2 * twos:2]
    slack = jnp.minimum(giver - 1, limit - sink)
    passed = jax.random.randint(jax.random.fold_in(key, 1), (twos,), 0, 1 << 20) % (slack + 1)
    sizes = sizes.at[1:1 + 2 * twos:2].set(giver - passed).at[2:2 + 2 * twos:2].set(sink + passed)
    return sizes[jax.random.permutation(jax.random.fold_in(key, 2), number_of)]


def bell_draw(key, extent, spread, most, pieces=(), kind=jnp.bfloat16):
    array = spread * jax.random.normal(key, extent, jnp.float32)
    if pieces:
        array = array * steps_of(key, extent, pieces, -0.22, 0.18)
    return jnp.clip(array, -most, most).astype(kind)


def setup_inputs(seed: int = 0) -> dict:
    arg_keys = jax.random.split(jax.random.key(seed), 9)
    return {
        "queries": draw_queries(jax.random.fold_in(arg_keys[8], 71), 0),
        "keys": draw_keys(jax.random.fold_in(arg_keys[8], 71), 0),
        "values": bell_draw(arg_keys[2], (TOKENS, KV_HEADS * HD), 1.0, 6.0, ((0, 32), (1, 4))),
        "prompt_keys": bell_draw(arg_keys[3], (PROMPT, KV_HEADS * HD), 1.0, 6.0, ((1, 4),)),
        "prompt_values": bell_draw(arg_keys[4], (PROMPT, KV_HEADS * HD), 1.0, 6.0, ((1, 4),)),
        "out_weight": bell_draw(arg_keys[5], (HEADS * HD, D), (HEADS * HD) ** -0.5, 0.09375, ((0, 4), (1, 32))),
        "out_grad": bell_draw(arg_keys[6], (TOKENS, D), 1.0, 6.0, ((0, 32),)),
        "lengths": jax.vmap(lambda own: ragged(own, DOCS, TOK_DEV, DOC_MOST, 2))(jax.random.split(arg_keys[7], N_DP)).reshape((N_DP, DOCS)).astype(jnp.int32),
    }


rope_base = 1000000.0


def doc_layout(lens, count):
    ends = jnp.cumsum(lens).astype(jnp.int32)
    starts = ends - lens
    index = jnp.arange(count, dtype=jnp.int32)
    segment = jnp.sum((index[:, None] >= ends[None, :]).astype(jnp.int32), axis=1).astype(jnp.int32)
    doc_ids = jnp.arange(lens.shape[0], dtype=jnp.int32)
    offset = jnp.sum(jnp.where(segment[:, None] == doc_ids[None, :], starts[None, :], 0), axis=1).astype(jnp.int32)
    return segment, index - offset


def rotate(field, position):
    half = HD // 2
    freq = rope_base ** (-2.0 * jnp.arange(half, dtype=jnp.float32) / HD)
    angle = position.astype(jnp.float32)[:, None] * freq[None, :]
    cosine = jnp.cos(angle)[:, None, :]
    sine = jnp.sin(angle)[:, None, :]
    first = field[..., :half].astype(jnp.float32)
    second = field[..., half:].astype(jnp.float32)
    return jnp.concatenate([first * cosine - second * sine, second * cosine + first * sine], axis=-1).astype(jnp.bfloat16)


def block_work(queries, keys, values, prompt_keys, prompt_values, out_weight, out_grad, lens):
    tok_rows = queries.shape[0]
    groups = HEADS // KV_HEADS
    scale = HD ** -0.5
    segment, position = doc_layout(lens, tok_rows)
    q_rot = rotate(queries.reshape(tok_rows, HEADS, HD), position).reshape(tok_rows, KV_HEADS, groups, HD)
    k_rot = rotate(keys.reshape(tok_rows, KV_HEADS, HD), position)
    key_all = jnp.concatenate([prompt_keys.reshape(PROMPT, KV_HEADS, HD), k_rot], axis=0)
    value_all = jnp.concatenate([prompt_values.reshape(PROMPT, KV_HEADS, HD), values.reshape(tok_rows, KV_HEADS, HD)], axis=0)
    index = jnp.arange(tok_rows, dtype=jnp.int32)
    own = (segment[:, None] == segment[None, :]) & (index[None, :] <= index[:, None])
    key_mask = jnp.concatenate([jnp.ones((tok_rows, PROMPT), dtype=bool), own], axis=1)
    scores = jnp.einsum('tkgd,skd->kgts', q_rot.astype(jnp.float32), key_all.astype(jnp.float32)) * scale
    scores = jnp.where(key_mask[None, None], scores, -1e30)
    shifted = jnp.exp(scores - jnp.max(scores, axis=-1, keepdims=True))
    shifted = jnp.where(key_mask[None, None], shifted, 0.0)
    probs = shifted / jnp.sum(shifted, axis=-1, keepdims=True)
    probs_b = probs.astype(jnp.bfloat16)
    attn = jnp.einsum('kgts,skd->tkgd', probs_b.astype(jnp.float32), value_all.astype(jnp.float32))
    attn = attn.astype(jnp.bfloat16).reshape(tok_rows, HEADS * HD)
    width = (HEADS // N_MP) * HD
    total = jnp.zeros((tok_rows, D), jnp.float32)
    for member in range(N_MP):
        partial_value = jnp.dot(attn[:, member * width:(member + 1) * width], out_weight[member * width:(member + 1) * width], preferred_element_type=jnp.float32)
        partial_value = lax.optimization_barrier(partial_value.astype(jnp.bfloat16))
        total = total + partial_value.astype(jnp.float32)
    mixed = total.astype(jnp.bfloat16)
    grad_attn = jnp.dot(out_grad, out_weight.T, preferred_element_type=jnp.float32).astype(jnp.bfloat16)
    grad_attn = grad_attn.reshape(tok_rows, KV_HEADS, groups, HD)
    value_grad = jnp.einsum('kgts,tkgd->skd', probs_b[..., :PROMPT].astype(jnp.float32), grad_attn.astype(jnp.float32))
    grad_probs = jnp.einsum('tkgd,skd->kgts', grad_attn.astype(jnp.float32), value_all.astype(jnp.float32))
    d_scores = probs * (grad_probs - jnp.sum(probs * grad_probs, axis=-1, keepdims=True)) * scale
    d_scores = d_scores.astype(jnp.bfloat16)
    key_grad = jnp.einsum('kgts,tkgd->skd', d_scores[..., :PROMPT].astype(jnp.float32), q_rot.astype(jnp.float32))
    return mixed, key_grad.reshape(PROMPT, KV_HEADS * HD), value_grad.reshape(PROMPT, KV_HEADS * HD)


def reference(queries, keys, values, prompt_keys, prompt_values, out_weight, out_grad, lengths):
    def one_block(block):
        start = (block * TOK_DEV).astype(jnp.int32)
        return block_work(
            lax.dynamic_slice_in_dim(queries, start, TOK_DEV, 0),
            lax.dynamic_slice_in_dim(keys, start, TOK_DEV, 0),
            lax.dynamic_slice_in_dim(values, start, TOK_DEV, 0),
            prompt_keys, prompt_values, out_weight,
            lax.dynamic_slice_in_dim(out_grad, start, TOK_DEV, 0),
            lengths[block])

    mixed, key_grad, value_grad = lax.map(one_block, jnp.arange(N_DP, dtype=jnp.int32))
    return mixed.reshape(TOKENS, D), jnp.sum(key_grad, axis=0), jnp.sum(value_grad, axis=0)
```

```python
import functools
import math

import jax
import jax.numpy as jnp
import numpy as np
from jax import lax
from jax.experimental import pallas as pl
from jax.experimental.pallas import tpu as pltpu
from jax.sharding import PartitionSpec as P

HD = 128
DOC_MOST = 320
ROPE_BASE = 1000000.0
TILE = 128
HALF = 512
UNIT = 256
MESH = pl.DeviceIdType.MESH
F32 = jnp.float32
BF16 = jnp.bfloat16


def pick(i, values):
    out = values[0]
    for k in range(1, len(values)):
        out = jnp.where(i == k, values[k], out)
    return out


STEPS = [
    [(0, 0, 0), (0, 1, 0), (0, -1, 0), (1, 0, 0)],
    [(0, 0, 1), (0, 0, -1), (0, 2, 0), (1, 0, 1)],
    [(1, 0, -1), (1, 1, 0), (1, -1, 0), (1, 0, 2)],
    [(0, 1, -1), (0, -1, 1), (1, -1, 1), (1, 1, -1)],
    [(0, -1, -1), (0, 2, 1), (1, -1, -1), (1, 1, 2)],
    [(0, 2, -1), (0, 1, 1), (1, -1, 2), (1, 1, 1)],
    [(0, 0, 2), (0, -1, 2), (1, 2, 0), (1, 2, -1)],
    [(0, 1, 2), (0, 2, 2), (1, 2, 1), (1, 2, 2)],
]
TICKS = [
    [(0, 1, 0), (0, -1, 0), (1, 0, 1), (1, 0, -1)],
    [(0, -1, 0), (0, 2, 0), (1, 0, -1), (1, 0, 2)],
    [(0, 2, 0), (0, 1, 0), (1, 0, 2), (1, 0, 1)],
    [(0, 0, -1), (0, -1, 1), (1, -1, 0), (1, 1, -1)],
    [(0, 1, -1), (0, 2, 1), (1, -1, 1), (1, 1, 2)],
]


def kernel(
    q_hbm, k_hbm, v_hbm, pk_hbm, pv_hbm, w_hbm, og_hbm, len_ref, freq_ref,
    out_hbm, kg_ref, vg_ref,
    wall, og, part, rbuf, zbuf, acc, attn, qrot, prob, qin, kin, kall, vall, cos_t, sin_t, start_t,
    in_sem, wsend, wrecv, csend, crecv, zsend, zrecv, osem,
):
    tok = q_hbm.shape[0]
    heads = q_hbm.shape[1] // HD
    prompt = pk_hbm.shape[0]
    n_tiles = tok // TILE
    scale = HD ** -0.5
    dp = lax.axis_index("dp")
    mp = lax.axis_index("mp")
    x0, y0, zl = dp % 4, (dp // 4) % 4, dp // 16
    zh, core = mp // 2, mp % 2

    def dpid(x, y, z):
        return z * 16 + y * 4 + x

    def pa(d):
        x = jnp.where(zl == 0, (x0 + d) % 4, x0)
        y = jnp.where(zl == 0, y0, (y0 + d) % 4)
        return (dpid(x, y, zl), mp)

    def pb(d):
        x = jnp.where(zl == 0, x0, (x0 + d) % 4)
        y = jnp.where(zl == 0, (y0 + d) % 4, y0)
        return (dpid(x, y, zl), mp)

    def slot(kind, da, db):
        x = (x0 + jnp.where(zl == 0, da, db) + 4) % 4
        y = (y0 + jnp.where(zl == 0, db, da) + 4) % 4
        t = jnp.where(kind == 0, zl, 1 - zl)
        return t * 16 + y * 4 + x

    a_up, a_dn, b_up, b_dn = pa(1), pa(3), pb(1), pb(3)
    z_peer = (dpid(x0, y0, 1 - zl), mp)
    c_peer = (dp, zh * 2 + 1 - core)
    far_peer = (dp, (1 - zh) * 2 + core)

    barrier = pltpu.get_barrier_semaphore()
    for peer in (a_up, a_dn, b_up, b_dn, z_peer, c_peer, far_peer):
        pl.semaphore_signal(barrier, inc=1, device_id=peer, device_id_type=MESH)

    me = slot(0, 0, 0)
    q_copy = pltpu.make_async_copy(q_hbm, qin, in_sem.at[0])
    k_copy = pltpu.make_async_copy(k_hbm, kin, in_sem.at[1])
    pk_copy = pltpu.make_async_copy(pk_hbm, kall.at[pl.ds(0, prompt)], in_sem.at[2])
    pv_copy = pltpu.make_async_copy(pv_hbm, vall.at[pl.ds(0, prompt)], in_sem.at[3])
    v_copy = pltpu.make_async_copy(v_hbm, vall.at[pl.ds(prompt, tok)], in_sem.at[4])
    w_copy = pltpu.make_async_copy(w_hbm, wall.at[me], in_sem.at[5])
    og_copy = pltpu.make_async_copy(og_hbm, og, in_sem.at[6])
    w_copy.start()
    for c in (k_copy, pk_copy, q_copy, pv_copy, v_copy):
        c.start()

    def rows(h):
        return pl.ds(h * HALF, HALF)

    def piece(s, h):
        return wall.at[s, rows(h)]

    def send(s, h, peer, n):
        pltpu.make_async_remote_copy(
            src_ref=piece(s, h), dst_ref=piece(s, h), send_sem=wsend.at[n], recv_sem=wrecv.at[s, h],
            device_id=peer, device_id_type=MESH,
        ).start()

    def arrived(s, h):
        pltpu.make_async_remote_copy(
            src_ref=piece(s, h), dst_ref=piece(s, h), send_sem=wsend.at[0], recv_sem=wrecv.at[s, h],
            device_id=z_peer, device_id_type=MESH,
        ).wait_recv()

    pl.semaphore_wait(barrier, 7)
    w_copy.wait()
    send(me, 0, z_peer, 0)
    send(me, 0, a_up, 1)
    send(me, 1, a_dn, 2)
    send(me, 0, b_up, 3)
    send(me, 1, b_dn, 4)
    send(me, 1, z_peer, 5)
    send(me, 1, a_up, 6)
    send(me, 0, a_dn, 7)
    send(me, 1, b_up, 8)
    send(me, 0, b_dn, 9)
    og_copy.start()

    t_col = lax.broadcasted_iota(jnp.int32, (tok, HD), 0)
    begin = jnp.zeros((tok, HD), jnp.int32)
    at = jnp.int32(0)
    for d in range(len_ref.shape[1]):
        begin = jnp.where(t_col >= at, at, begin)
        at = at + len_ref[0, d]
    start_t[...] = begin
    angle = (t_col - begin).astype(F32) * freq_ref[0:1, :]
    cos_t[...] = jnp.cos(angle)
    sin_t[...] = jnp.sin(angle) * freq_ref[1:2, :]

    def rotated(field, lo, n):
        f = field.astype(F32)
        return (f * cos_t[pl.ds(lo, n), :] + pltpu.roll(f, HD // 2, 1) * sin_t[pl.ds(lo, n), :]).astype(BF16)

    k_copy.wait()
    kall[pl.ds(prompt, tok), :] = rotated(kin[...], 0, tok)
    for c in (pk_copy, q_copy, pv_copy, v_copy):
        c.wait()
    acc[...] = jnp.zeros_like(acc)

    def attention(i):
        lo = max(0, i - (DOC_MOST + TILE - 2) // TILE) * TILE
        n = (i + 1) * TILE - lo
        r = pl.ds(i * TILE, TILE)
        nt = (((1,), (1,)), ((), ()))

        def head(h, carry):
            lanes = pl.ds(pl.multiple_of(h * HD, HD), HD)
            q = rotated(qin[r, lanes], i * TILE, TILE)
            qrot[r, lanes] = q
            s_p = lax.dot_general(q, kall[pl.ds(0, prompt), :], nt, preferred_element_type=F32)
            s_t = lax.dot_general(q, kall[pl.ds(prompt + lo, n), :], nt, preferred_element_type=F32)
            col = lax.broadcasted_iota(jnp.int32, (TILE, n), 1) + lo
            row = lax.broadcasted_iota(jnp.int32, (TILE, n), 0) + i * TILE
            seen = (col <= row) & (col >= start_t[r, 0:1])
            s_t = jnp.where(seen, s_t, -1e30)
            top = jnp.maximum(jnp.max(s_p, axis=1, keepdims=True), jnp.max(s_t, axis=1, keepdims=True))
            e_p = jnp.exp((s_p - top) * scale)
            e_t = jnp.exp((s_t - top) * scale)
            inv = 1.0 / (jnp.sum(e_p, axis=1, keepdims=True) + jnp.sum(e_t, axis=1, keepdims=True))
            o = jnp.dot(e_p.astype(BF16), vall[pl.ds(0, prompt), :], preferred_element_type=F32)
            o = o + jnp.dot(e_t.astype(BF16), vall[pl.ds(prompt + lo, n), :], preferred_element_type=F32)
            attn[r, lanes] = (o * inv).astype(BF16)
            prob[r, lanes] = (e_p * inv).astype(BF16)
            return carry

        lax.fori_loop(0, heads, head, 0, unroll=2)

    attention(0)
    attention(1)
    attention(2)

    arrived(slot(0, -1, 0), 0)
    send(slot(0, -1, 0), 0, a_up, 10)
    arrived(slot(0, 1, 0), 1)
    send(slot(0, 1, 0), 1, a_dn, 11)
    other = slot(1, 0, 0)
    arrived(other, 0)
    send(other, 0, b_up, 12)
    arrived(other, 1)
    send(other, 1, b_dn, 13)
    send(other, 1, b_up, 14)
    send(other, 0, b_dn, 15)
    send(other, 0, a_up, 16)
    send(other, 1, a_dn, 17)
    send(other, 1, a_up, 18)
    send(other, 0, a_dn, 19)
    attention(3)
    attention(4)
    arrived(slot(1, 0, -1), 0)
    send(slot(1, 0, -1), 0, b_up, 20)
    arrived(slot(1, 0, 1), 1)
    send(slot(1, 0, 1), 1, b_dn, 21)
    og_copy.wait()

    def slot_of(step, table, j):
        kind = 0 if j < 2 else 1
        return slot(kind, pick(step, [t[j][1] for t in table]), pick(step, [t[j][2] for t in table]))

    def tick(t):
        n = 22 + 8 * t
        up, dn = slot_of(t, TICKS, 0), slot_of(t, TICKS, 1)
        up2, dn2 = slot_of(t, TICKS, 2), slot_of(t, TICKS, 3)
        for h in range(2):
            send(up, h, b_up, n + h)
            send(dn, h, b_dn, n + 2 + h)
            send(up2, h, a_up, n + 4 + h)
            send(dn2, h, a_dn, n + 6 + h)

    def unit(step, j):
        i = step * 4 + j
        flat = [u for four in STEPS for u in four]
        return slot(pick(i, [u[0] for u in flat]), pick(i, [u[1] for u in flat]), pick(i, [u[2] for u in flat]))

    def index_of(s):
        return (s // 16) * 8 + ((s // 4) % 2) * 4 + s % 4

    def core_copy(s):
        n = index_of(s)
        return pltpu.make_async_remote_copy(
            src_ref=part.at[s], dst_ref=rbuf.at[n], send_sem=csend.at[n], recv_sem=crecv.at[n],
            device_id=c_peer, device_id_type=MESH,
        )

    def far_copy(s):
        n = index_of(s) % 8
        return pltpu.make_async_remote_copy(
            src_ref=part.at[s], dst_ref=zbuf.at[n], send_sem=zsend.at[n], recv_sem=zrecv.at[n],
            device_id=far_peer, device_id_type=MESH,
        )

    def process(s):
        part[s] = jnp.dot(attn[...], wall[s], preferred_element_type=F32).astype(BF16)

        @pl.when((s // 8) % 2 != core)
        def _():
            core_copy(s).start()

        g = og[:, pl.ds(pl.multiple_of(s * UNIT, UNIT), UNIT)]
        for b in range(acc.shape[1] // UNIT):
            w = wall[s, b * UNIT:(b + 1) * UNIT, :]
            acc[:, b * UNIT:(b + 1) * UNIT] += lax.dot_general(
                g, w, (((1,), (1,)), ((), ())), preferred_element_type=F32
            )

    def combine(s):
        @pl.when((s // 8) % 2 == core)
        def _():
            n = index_of(s)
            core_copy(s).wait_recv()
            part[s] = (part[s].astype(F32) + rbuf[n].astype(F32)).astype(BF16)

            @pl.when(s // 16 != zh)
            def _():
                far_copy(s).start()

    def both(s):
        arrived(s, 0)
        arrived(s, 1)

    def step_body(step, carry):
        @pl.when(step == 0)
        def _():
            arrived(slot(0, -1, 0), 1)
            arrived(slot(0, 1, 0), 0)

        @pl.when(step == 1)
        def _():
            both(slot(0, 0, 1))
            both(slot(0, 0, -1))
            both(slot(0, 2, 0))
            arrived(slot(1, 0, -1), 1)
            arrived(slot(1, 0, 1), 0)
            tick(0)

        @pl.when(step == 2)
        def _():
            both(slot(1, 1, 0))
            both(slot(1, -1, 0))
            both(slot(1, 0, 2))
            tick(1)

        @pl.when(step >= 3)
        def _():
            for j in range(4):
                both(unit(step, j))

            @pl.when(step <= 5)
            def _():
                tick(step - 1)

        def one(j, c):
            process(unit(step, j))
            return c

        lax.fori_loop(0, 4, one, 0)

        @pl.when(step > 0)
        def _():
            def two(j, c):
                combine(unit(step - 1, j))
                return c

            lax.fori_loop(0, 4, two, 0)

        return carry

    lax.fori_loop(0, 8, step_body, 0)

    def last(j, c):
        combine(unit(7, j))
        return c

    lax.fori_loop(0, 4, last, 0)

    tn = (((0,), (0,)), ((), ()))
    nt = (((1,), (1,)), ((), ()))
    kg_ref[...] = jnp.zeros_like(kg_ref)
    vg_ref[...] = jnp.zeros_like(vg_ref)

    def grads(h, c):
        lanes = pl.ds(pl.multiple_of(h * HD, HD), HD)
        g = acc[:, lanes].astype(BF16)
        p = prob[:, lanes]
        delta = jnp.sum(g.astype(F32) * attn[:, lanes].astype(F32), axis=1, keepdims=True)
        gp = lax.dot_general(g, vall[pl.ds(0, prompt), :], nt, preferred_element_type=F32)
        ds = (p.astype(F32) * (gp - delta) * scale).astype(BF16)
        kg_ref[...] += lax.dot_general(ds, qrot[:, lanes], tn, preferred_element_type=F32)
        vg_ref[...] += lax.dot_general(p, g, tn, preferred_element_type=F32)
        return c

    lax.fori_loop(0, heads, grads, 0)

    def out_copy(n):
        s = zh * 16 + core * 8 + n
        return pltpu.make_async_copy(
            part.at[s], out_hbm.at[:, pl.ds(pl.multiple_of(n * UNIT, UNIT), UNIT)], osem.at[n]
        )

    def finish(j, c):
        s = unit(j // 4, j % 4)

        @pl.when(((s // 8) % 2 == core) & (s // 16 == zh))
        def _():
            n = index_of(s) % 8
            far_copy(s).wait_recv()
            part[s] = (part[s].astype(F32) + zbuf[n].astype(F32)).astype(BF16)
            out_copy(n).start()

        return c

    lax.fori_loop(0, 32, finish, 0)

    def drain(n, c):
        pltpu.make_async_remote_copy(
            src_ref=piece(0, 0), dst_ref=piece(0, 0), send_sem=wsend.at[n], recv_sem=wrecv.at[0, 0],
            device_id=z_peer, device_id_type=MESH,
        ).wait_send()
        return c

    lax.fori_loop(0, 62, drain, 0)

    def drain_parts(s, c):
        @pl.when((s // 8) % 2 != core)
        def _():
            core_copy(s).wait_send()

        @pl.when(((s // 8) % 2 == core) & (s // 16 != zh))
        def _():
            far_copy(s).wait_send()

        return c

    lax.fori_loop(0, 32, drain_parts, 0)

    def drain_out(n, c):
        out_copy(n).wait()
        return c

    lax.fori_loop(0, 8, drain_out, 0)


def split_up(x, dim, length):
    dims = x.shape
    parts = x.reshape(*dims[:dim], length, dims[dim] // length, *dims[dim + 1:])
    return jnp.moveaxis(parts, dim, 0)


def sum_at_owner(x, axis, dim):
    length = lax.axis_size(axis)
    parts = lax.all_to_all(split_up(x, dim, length), axis, 0, 0, tiled=True)
    return jnp.sum(parts.astype(F32), axis=0)


def per_device(queries, keys, values, prompt_keys, prompt_values, out_weight, out_grad, lengths):
    tok, width = queries.shape
    prompt = prompt_keys.shape[0]
    n_dp = lax.axis_size("dp")
    half = HD // 2
    freq = ROPE_BASE ** (-2.0 * np.arange(half) / HD)
    table = np.zeros((8, HD), np.float32)
    table[0] = np.concatenate([freq, freq])
    table[1] = np.concatenate([-np.ones(half), np.ones(half)])
    anywhere = pl.BlockSpec(memory_space=pl.ANY)
    vmem = pl.BlockSpec(memory_space=pltpu.VMEM)
    dma = pltpu.SemaphoreType.DMA
    mixed, key_grad, value_grad = pl.pallas_call(
        kernel,
        out_shape=(
            jax.ShapeDtypeStruct((tok, 8 * UNIT), BF16),
            jax.ShapeDtypeStruct((prompt, HD), F32),
            jax.ShapeDtypeStruct((prompt, HD), F32),
        ),
        in_specs=[anywhere] * 7 + [pl.BlockSpec(memory_space=pltpu.SMEM), vmem],
        out_specs=(anywhere, vmem, vmem),
        scratch_shapes=[
            pltpu.VMEM((n_dp, width, UNIT), BF16),
            pltpu.VMEM((tok, n_dp * UNIT), BF16),
            pltpu.VMEM((n_dp, tok, UNIT), BF16),
            pltpu.VMEM((16, tok, UNIT), BF16),
            pltpu.VMEM((8, tok, UNIT), BF16),
            pltpu.VMEM((tok, width), F32),
            pltpu.VMEM((tok, width), BF16),
            pltpu.VMEM((tok, width), BF16),
            pltpu.VMEM((tok, width), BF16),
            pltpu.VMEM((tok, width), BF16),
            pltpu.VMEM((tok, HD), BF16),
            pltpu.VMEM((prompt + tok, HD), BF16),
            pltpu.VMEM((prompt + tok, HD), BF16),
            pltpu.VMEM((tok, HD), F32),
            pltpu.VMEM((tok, HD), F32),
            pltpu.VMEM((tok, HD), jnp.int32),
            dma((7,)),
            dma((62,)),
            dma((n_dp, 2)),
            dma((16,)),
            dma((16,)),
            dma((8,)),
            dma((8,)),
            dma((8,)),
        ],
        compiler_params=pltpu.CompilerParams(
            collective_id=0, has_side_effects=True, vmem_limit_bytes=62 * 1024 * 1024
        ),
    )(queries, keys, values, prompt_keys, prompt_values, out_weight, out_grad, lengths, jnp.asarray(table))
    both = jnp.concatenate([key_grad, value_grad], axis=1).astype(BF16)
    owned = sum_at_owner(both, "dp", 0)
    return mixed, owned[:, :HD], owned[:, HD:]


def solution(mesh):
    in_specs = (
        P("dp", "mp"),
        P("dp", "mp"),
        P("dp", "mp"),
        P(None, "mp"),
        P(None, "mp"),
        P("mp", "dp"),
        P("dp", None),
        P("dp", None),
    )
    out_specs = (P("dp", "mp"), P("dp", "mp"), P("dp", "mp"))
    return jax.shard_map(
        per_device, mesh=mesh, in_specs=in_specs, out_specs=out_specs, check_vma=False
    )
```

```python
import functools
import math

import jax
import jax.numpy as jnp
import numpy as np
from jax import lax
from jax.experimental import pallas as pl
from jax.experimental.pallas import tpu as pltpu
from jax.sharding import PartitionSpec as P

HD = 128
DOC_MOST = 320
ROPE_BASE = 1000000.0
TILE = 128
HALF = 512
UNIT = 256
MESH = pl.DeviceIdType.MESH
F32 = jnp.float32
BF16 = jnp.bfloat16


def pick(i, values):
    out = values[0]
    for k in range(1, len(values)):
        out = jnp.where(i == k, values[k], out)
    return out


STEPS = [
    [(0, 0, 0), (0, 1, 0), (0, -1, 0), (1, 0, 0)],
    [(0, 0, 1), (0, 0, -1), (0, 2, 0), (1, 0, 1)],
    [(1, 0, -1), (1, 1, 0), (1, -1, 0), (1, 0, 2)],
    [(0, 1, -1), (0, -1, 1), (1, -1, 1), (1, 1, -1)],
    [(0, -1, -1), (0, 2, 1), (1, -1, -1), (1, 1, 2)],
    [(0, 2, -1), (0, 1, 1), (1, -1, 2), (1, 1, 1)],
    [(0, 0, 2), (0, -1, 2), (1, 2, 0), (1, 2, -1)],
    [(0, 1, 2), (0, 2, 2), (1, 2, 1), (1, 2, 2)],
]
TICKS = [
    [(0, 1, 0), (0, -1, 0), (1, 0, 1), (1, 0, -1)],
    [(0, -1, 0), (0, 2, 0), (1, 0, -1), (1, 0, 2)],
    [(0, 2, 0), (0, 1, 0), (1, 0, 2), (1, 0, 1)],
    [(0, 0, -1), (0, -1, 1), (1, -1, 0), (1, 1, -1)],
    [(0, 1, -1), (0, 2, 1), (1, -1, 1), (1, 1, 2)],
]


def kernel(
    q_hbm, k_hbm, v_hbm, pk_hbm, pv_hbm, w_hbm, og_hbm, len_ref, freq_ref,
    own_hbm, far_hbm, g_out,
    wall, og, part, rbuf, kg, vg, gsend, grecv, acc, attn, qrot, prob, qin, kin, kall, vall, cos_t, sin_t, start_t,
    in_sem, wsend, wrecv, csend, crecv, zsend, zrecv, osem, gssem, grsem,
):
    tok = q_hbm.shape[0]
    heads = q_hbm.shape[1] // HD
    prompt = pk_hbm.shape[0]
    n_tiles = tok // TILE
    scale = HD ** -0.5
    dp = lax.axis_index("dp")
    mp = lax.axis_index("mp")
    x0, y0, zl = dp % 4, (dp // 4) % 4, dp // 16
    zh, core = mp // 2, mp % 2

    def dpid(x, y, z):
        return z * 16 + y * 4 + x

    def pa(d):
        x = jnp.where(zl == 0, (x0 + d) % 4, x0)
        y = jnp.where(zl == 0, y0, (y0 + d) % 4)
        return (dpid(x, y, zl), mp)

    def pb(d):
        x = jnp.where(zl == 0, x0, (x0 + d) % 4)
        y = jnp.where(zl == 0, (y0 + d) % 4, y0)
        return (dpid(x, y, zl), mp)

    def slot(kind, da, db):
        x = (x0 + jnp.where(zl == 0, da, db) + 4) % 4
        y = (y0 + jnp.where(zl == 0, db, da) + 4) % 4
        t = jnp.where(kind == 0, zl, 1 - zl)
        return t * 16 + y * 4 + x

    a_up, a_dn, b_up, b_dn = pa(1), pa(3), pb(1), pb(3)
    z_peer = (dpid(x0, y0, 1 - zl), mp)
    c_peer = (dp, zh * 2 + 1 - core)
    far_peer = (dp, (1 - zh) * 2 + core)

    barrier = pltpu.get_barrier_semaphore()
    for peer in (a_up, a_dn, b_up, b_dn, z_peer, c_peer, far_peer):
        pl.semaphore_signal(barrier, inc=1, device_id=peer, device_id_type=MESH)

    me = slot(0, 0, 0)
    q_copy = pltpu.make_async_copy(q_hbm, qin, in_sem.at[0])
    k_copy = pltpu.make_async_copy(k_hbm, kin, in_sem.at[1])
    pk_copy = pltpu.make_async_copy(pk_hbm, kall.at[pl.ds(0, prompt)], in_sem.at[2])
    pv_copy = pltpu.make_async_copy(pv_hbm, vall.at[pl.ds(0, prompt)], in_sem.at[3])
    v_copy = pltpu.make_async_copy(v_hbm, vall.at[pl.ds(prompt, tok)], in_sem.at[4])
    w_copy = pltpu.make_async_copy(w_hbm, wall.at[me], in_sem.at[5])
    og_copy = pltpu.make_async_copy(og_hbm, og, in_sem.at[6])
    w_copy.start()
    for c in (k_copy, pk_copy, q_copy, pv_copy, v_copy):
        c.start()

    def rows(h):
        return pl.ds(h * HALF, HALF)

    def piece(s, h):
        return wall.at[s, rows(h)]

    def send_own(h, peer, n):
        pltpu.make_async_remote_copy(
            src_ref=w_hbm.at[rows(h)], dst_ref=piece(me, h), send_sem=wsend.at[n], recv_sem=wrecv.at[me, h],
            device_id=peer, device_id_type=MESH,
        ).start()

    def send(s, h, peer, n):
        pltpu.make_async_remote_copy(
            src_ref=piece(s, h), dst_ref=piece(s, h), send_sem=wsend.at[n], recv_sem=wrecv.at[s, h],
            device_id=peer, device_id_type=MESH,
        ).start()

    def arrived(s, h):
        pltpu.make_async_remote_copy(
            src_ref=piece(s, h), dst_ref=piece(s, h), send_sem=wsend.at[0], recv_sem=wrecv.at[s, h],
            device_id=z_peer, device_id_type=MESH,
        ).wait_recv()

    pl.semaphore_wait(barrier, 7)
    send_own(0, z_peer, 0)
    send_own(0, a_up, 1)
    send_own(1, a_dn, 2)
    send_own(0, b_up, 3)
    send_own(1, b_dn, 4)
    send_own(1, z_peer, 5)
    send_own(1, a_up, 6)
    send_own(0, a_dn, 7)
    send_own(1, b_up, 8)
    send_own(0, b_dn, 9)
    og_copy.start()

    t_col = lax.broadcasted_iota(jnp.int32, (tok, HD), 0)
    begin = jnp.zeros((tok, HD), jnp.int32)
    at = jnp.int32(0)
    for d in range(len_ref.shape[1]):
        begin = jnp.where(t_col >= at, at, begin)
        at = at + len_ref[0, d]
    start_t[...] = begin
    angle = (t_col - begin).astype(F32) * freq_ref[0:1, :]
    cos_t[...] = jnp.cos(angle)
    sin_t[...] = jnp.sin(angle) * freq_ref[1:2, :]

    def rotated(field, lo, n):
        f = field.astype(F32)
        return (f * cos_t[pl.ds(lo, n), :] + pltpu.roll(f, HD // 2, 1) * sin_t[pl.ds(lo, n), :]).astype(BF16)

    k_copy.wait()
    kall[pl.ds(prompt, tok), :] = rotated(kin[...], 0, tok)
    for c in (pk_copy, q_copy, pv_copy, v_copy, w_copy):
        c.wait()
    acc[...] = jnp.zeros_like(acc)

    def attention(i):
        lo = max(0, i - (DOC_MOST + TILE - 2) // TILE) * TILE
        n = (i + 1) * TILE - lo
        r = pl.ds(i * TILE, TILE)
        nt = (((1,), (1,)), ((), ()))

        def head(h, carry):
            lanes = pl.ds(pl.multiple_of(h * HD, HD), HD)
            q = rotated(qin[r, lanes], i * TILE, TILE)
            qrot[r, lanes] = q
            s_p = lax.dot_general(q, kall[pl.ds(0, prompt), :], nt, preferred_element_type=F32)
            s_t = lax.dot_general(q, kall[pl.ds(prompt + lo, n), :], nt, preferred_element_type=F32)
            col = lax.broadcasted_iota(jnp.int32, (TILE, n), 1) + lo
            row = lax.broadcasted_iota(jnp.int32, (TILE, n), 0) + i * TILE
            seen = (col <= row) & (col >= start_t[r, 0:1])
            s_t = jnp.where(seen, s_t, -1e30)
            top = jnp.maximum(jnp.max(s_p, axis=1, keepdims=True), jnp.max(s_t, axis=1, keepdims=True))
            e_p = jnp.exp((s_p - top) * scale)
            e_t = jnp.exp((s_t - top) * scale)
            inv = 1.0 / (jnp.sum(e_p, axis=1, keepdims=True) + jnp.sum(e_t, axis=1, keepdims=True))
            o = jnp.dot(e_p.astype(BF16), vall[pl.ds(0, prompt), :], preferred_element_type=F32)
            o = o + jnp.dot(e_t.astype(BF16), vall[pl.ds(prompt + lo, n), :], preferred_element_type=F32)
            attn[r, lanes] = (o * inv).astype(BF16)
            prob[r, lanes] = (e_p * inv).astype(BF16)
            return carry

        lax.fori_loop(0, heads, head, 0, unroll=2)

    attention(0)
    attention(1)
    attention(2)

    arrived(slot(0, -1, 0), 0)
    send(slot(0, -1, 0), 0, a_up, 10)
    arrived(slot(0, 1, 0), 1)
    send(slot(0, 1, 0), 1, a_dn, 11)
    other = slot(1, 0, 0)
    arrived(other, 0)
    send(other, 0, b_up, 12)
    arrived(other, 1)
    send(other, 1, b_dn, 13)
    send(other, 1, b_up, 14)
    send(other, 0, b_dn, 15)
    send(other, 0, a_up, 16)
    send(other, 1, a_dn, 17)
    send(other, 1, a_up, 18)
    send(other, 0, a_dn, 19)
    attention(3)
    attention(4)
    arrived(slot(1, 0, -1), 0)
    send(slot(1, 0, -1), 0, b_up, 20)
    arrived(slot(1, 0, 1), 1)
    send(slot(1, 0, 1), 1, b_dn, 21)
    og_copy.wait()

    def slot_of(step, table, j):
        kind = 0 if j < 2 else 1
        return slot(kind, pick(step, [t[j][1] for t in table]), pick(step, [t[j][2] for t in table]))

    def tick(t):
        n = 22 + 8 * t
        up, dn = slot_of(t, TICKS, 0), slot_of(t, TICKS, 1)
        up2, dn2 = slot_of(t, TICKS, 2), slot_of(t, TICKS, 3)
        for h in range(2):
            send(up, h, b_up, n + h)
            send(dn, h, b_dn, n + 2 + h)
            send(up2, h, a_up, n + 4 + h)
            send(dn2, h, a_dn, n + 6 + h)

    def unit(step, j):
        i = step * 4 + jnp.where((step >= 3) & (zl == zh), (j + 2) % 4, j)
        flat = [u for four in STEPS for u in four]
        return slot(pick(i, [u[0] for u in flat]), pick(i, [u[1] for u in flat]), pick(i, [u[2] for u in flat]))

    def index_of(s):
        return (s // 16) * 8 + ((s // 4) % 2) * 4 + s % 4

    def core_copy(s):
        n = index_of(s)
        return pltpu.make_async_remote_copy(
            src_ref=part.at[s], dst_ref=rbuf.at[n], send_sem=csend.at[n], recv_sem=crecv.at[n],
            device_id=c_peer, device_id_type=MESH,
        )

    def far_copy(s):
        n = index_of(s) % 8
        return pltpu.make_async_remote_copy(
            src_ref=part.at[s], dst_ref=far_hbm.at[:, columns(n)], send_sem=zsend.at[n], recv_sem=zrecv.at[n],
            device_id=far_peer, device_id_type=MESH,
        )

    def columns(n):
        return pl.ds(pl.multiple_of(n * UNIT, UNIT), UNIT)

    def own_copy(s):
        n = index_of(s) % 8
        return pltpu.make_async_copy(part.at[s], own_hbm.at[:, columns(n)], osem.at[n])

    def process(s):
        part[s] = jnp.dot(attn[...], wall[s], preferred_element_type=F32).astype(BF16)

        @pl.when((s // 8) % 2 != core)
        def _():
            core_copy(s).start()

        g = og[:, pl.ds(pl.multiple_of(s * UNIT, UNIT), UNIT)]
        for b in range(acc.shape[1] // UNIT):
            w = wall[s, b * UNIT:(b + 1) * UNIT, :]
            acc[:, b * UNIT:(b + 1) * UNIT] += lax.dot_general(
                g, w, (((1,), (1,)), ((), ())), preferred_element_type=F32
            )

    def combine(s):
        @pl.when((s // 8) % 2 == core)
        def _():
            n = index_of(s)
            core_copy(s).wait_recv()
            part[s] = (part[s].astype(F32) + rbuf[n].astype(F32)).astype(BF16)

            @pl.when(s // 16 != zh)
            def _():
                far_copy(s).start()

            @pl.when(s // 16 == zh)
            def _():
                own_copy(s).start()

    def both(s):
        arrived(s, 0)
        arrived(s, 1)

    def step_body(step, carry):
        @pl.when(step == 0)
        def _():
            arrived(slot(0, -1, 0), 1)
            arrived(slot(0, 1, 0), 0)

        @pl.when(step == 1)
        def _():
            both(slot(0, 0, 1))
            both(slot(0, 0, -1))
            both(slot(0, 2, 0))
            arrived(slot(1, 0, -1), 1)
            arrived(slot(1, 0, 1), 0)
            tick(0)

        @pl.when(step == 2)
        def _():
            both(slot(1, 1, 0))
            both(slot(1, -1, 0))
            both(slot(1, 0, 2))
            tick(1)

        @pl.when((step >= 3) & (step <= 5))
        def _():
            for j in range(4):
                both(unit(step, j))
            tick(step - 1)

        def one(j, c):
            s = unit(step, j)

            @pl.when(step >= 6)
            def _():
                both(s)

            process(s)

            @pl.when(j > 0)
            def _():
                combine(unit(step, j - 1))

            return c

        lax.fori_loop(0, 4, one, 0)
        combine(unit(step, 3))
        return carry

    lax.fori_loop(0, 8, step_body, 0)

    tn = (((0,), (0,)), ((), ()))
    nt = (((1,), (1,)), ((), ()))
    kg[...] = jnp.zeros_like(kg)
    vg[...] = jnp.zeros_like(vg)

    def grads(h, c):
        lanes = pl.ds(pl.multiple_of(h * HD, HD), HD)
        g = acc[:, lanes].astype(BF16)
        p = prob[:, lanes]
        delta = jnp.sum(g.astype(F32) * attn[:, lanes].astype(F32), axis=1, keepdims=True)
        gp = lax.dot_general(g, vall[pl.ds(0, prompt), :], nt, preferred_element_type=F32)
        ds = (p.astype(F32) * (gp - delta) * scale).astype(BF16)
        kg[...] += lax.dot_general(ds, qrot[:, lanes], tn, preferred_element_type=F32)
        vg[...] += lax.dot_general(p, g, tn, preferred_element_type=F32)
        return c

    lax.fori_loop(0, heads, grads, 0)

    n_dp = gsend.shape[0]
    own_rows = prompt // n_dp
    gsend[:, 0:own_rows, :] = kg[...].reshape(n_dp, own_rows, HD)
    gsend[:, own_rows:2 * own_rows, :] = vg[...].reshape(n_dp, own_rows, HD)

    def grad_copy(j):
        return pltpu.make_async_remote_copy(
            src_ref=gsend.at[(dp + j) % n_dp], dst_ref=grecv.at[dp], send_sem=gssem.at[j], recv_sem=grsem.at[dp],
            device_id=((dp + j) % n_dp, mp), device_id_type=MESH,
        )

    def grad_send(j, c):
        grad_copy(j).start()
        return c

    lax.fori_loop(1, n_dp, grad_send, 0)
    grecv[dp] = gsend[dp]

    def drain(n, c):
        pltpu.make_async_remote_copy(
            src_ref=piece(0, 0), dst_ref=piece(0, 0), send_sem=wsend.at[n], recv_sem=wrecv.at[0, 0],
            device_id=z_peer, device_id_type=MESH,
        ).wait_send()
        return c

    lax.fori_loop(0, 62, drain, 0)

    def drain_parts(s, c):
        @pl.when((s // 8) % 2 != core)
        def _():
            core_copy(s).wait_send()

        @pl.when(((s // 8) % 2 == core) & (s // 16 == zh))
        def _():
            own_copy(s).wait()

        return c

    lax.fori_loop(0, n_dp, drain_parts, 0)

    def grad_wait(j, c):
        src = (dp + j) % n_dp
        pltpu.make_async_remote_copy(
            src_ref=gsend.at[src], dst_ref=grecv.at[src], send_sem=gssem.at[j], recv_sem=grsem.at[src],
            device_id=(src, mp), device_id_type=MESH,
        ).wait()
        return c

    lax.fori_loop(1, n_dp, grad_wait, 0)
    g_out[...] = jnp.sum(grecv[...], axis=0)

    def far_wait(n, c):
        far_copy((1 - zh) * 16 + core * 8 + n).wait()
        return c

    lax.fori_loop(0, 8, far_wait, 0)


def finish(own_ref, far_ref, g_ref, out_ref, kg_ref, vg_ref):
    out_ref[...] = (own_ref[...].astype(F32) + far_ref[...].astype(F32)).astype(BF16)
    n = kg_ref.shape[0]
    kg_ref[...] = g_ref[0:n, :]
    vg_ref[...] = g_ref[n:2 * n, :]


def per_device(queries, keys, values, prompt_keys, prompt_values, out_weight, out_grad, lengths):
    tok, width = queries.shape
    prompt = prompt_keys.shape[0]
    n_dp = lax.axis_size("dp")
    own_rows = prompt // n_dp
    half = HD // 2
    freq = ROPE_BASE ** (-2.0 * np.arange(half) / HD)
    table = np.zeros((8, HD), np.float32)
    table[0] = np.concatenate([freq, freq])
    table[1] = np.concatenate([-np.ones(half), np.ones(half)])
    anywhere = pl.BlockSpec(memory_space=pl.ANY)
    vmem = pl.BlockSpec(memory_space=pltpu.VMEM)
    dma = pltpu.SemaphoreType.DMA
    own, far, grad = pl.pallas_call(
        kernel,
        out_shape=(
            jax.ShapeDtypeStruct((tok, 8 * UNIT), BF16),
            jax.ShapeDtypeStruct((tok, 8 * UNIT), BF16),
            jax.ShapeDtypeStruct((2 * own_rows, HD), F32),
        ),
        in_specs=[anywhere] * 7 + [pl.BlockSpec(memory_space=pltpu.SMEM), vmem],
        out_specs=(anywhere, anywhere, vmem),
        scratch_shapes=[
            pltpu.VMEM((n_dp, width, UNIT), BF16),
            pltpu.VMEM((tok, n_dp * UNIT), BF16),
            pltpu.VMEM((n_dp, tok, UNIT), BF16),
            pltpu.VMEM((16, tok, UNIT), BF16),
            pltpu.VMEM((prompt, HD), F32),
            pltpu.VMEM((prompt, HD), F32),
            pltpu.VMEM((n_dp, 2 * own_rows, HD), F32),
            pltpu.VMEM((n_dp, 2 * own_rows, HD), F32),
            pltpu.VMEM((tok, width), F32),
            pltpu.VMEM((tok, width), BF16),
            pltpu.VMEM((tok, width), BF16),
            pltpu.VMEM((tok, width), BF16),
            pltpu.VMEM((tok, width), BF16),
            pltpu.VMEM((tok, HD), BF16),
            pltpu.VMEM((prompt + tok, HD), BF16),
            pltpu.VMEM((prompt + tok, HD), BF16),
            pltpu.VMEM((tok, HD), F32),
            pltpu.VMEM((tok, HD), F32),
            pltpu.VMEM((tok, HD), jnp.int32),
            dma((7,)),
            dma((62,)),
            dma((n_dp, 2)),
            dma((16,)),
            dma((16,)),
            dma((8,)),
            dma((8,)),
            dma((8,)),
            dma((n_dp,)),
            dma((n_dp,)),
        ],
        compiler_params=pltpu.CompilerParams(
            collective_id=0, has_side_effects=True, vmem_limit_bytes=62 * 1024 * 1024
        ),
    )(queries, keys, values, prompt_keys, prompt_values, out_weight, out_grad, lengths, jnp.asarray(table))
    block = 2 * TILE if tok % (2 * TILE) == 0 else TILE
    wide = pl.BlockSpec((block, 8 * UNIT), lambda i: (i, 0))
    few = pl.BlockSpec((own_rows, HD), lambda i: (0, 0))
    return pl.pallas_call(
        finish,
        grid=(tok // block,),
        out_shape=(
            jax.ShapeDtypeStruct((tok, 8 * UNIT), BF16),
            jax.ShapeDtypeStruct((own_rows, HD), F32),
            jax.ShapeDtypeStruct((own_rows, HD), F32),
        ),
        in_specs=[wide, wide, pl.BlockSpec((2 * own_rows, HD), lambda i: (0, 0))],
        out_specs=(wide, few, few),
    )(own, far, grad)


def solution(mesh):
    in_specs = (
        P("dp", "mp"),
        P("dp", "mp"),
        P("dp", "mp"),
        P(None, "mp"),
        P(None, "mp"),
        P("mp", "dp"),
        P("dp", None),
        P("dp", None),
    )
    out_specs = (P("dp", "mp"), P("dp", "mp"), P("dp", "mp"))
    return jax.shard_map(
        per_device, mesh=mesh, in_specs=in_specs, out_specs=out_specs, check_vma=False
    )
```

```python
import functools
import math

import jax
import jax.numpy as jnp
import numpy as np
from jax import lax
from jax.experimental import pallas as pl
from jax.experimental.pallas import tpu as pltpu
from jax.sharding import PartitionSpec as P

HD = 128
DOC_MOST = 320
ROPE_BASE = 1000000.0
TILE = 128
HALF = 512
UNIT = 256
MESH = pl.DeviceIdType.MESH
F32 = jnp.float32
BF16 = jnp.bfloat16


def pick(i, values):
    out = values[0]
    for k in range(1, len(values)):
        out = jnp.where(i == k, values[k], out)
    return out


STEPS = [
    [(0, 0, 0), (0, 1, 0), (0, -1, 0), (1, 0, 0)],
    [(0, 0, 1), (0, 0, -1), (0, 2, 0), (1, 0, 1)],
    [(1, 0, -1), (1, 1, 0), (1, -1, 0), (1, 0, 2)],
    [(0, 1, -1), (0, -1, 1), (1, -1, 1), (1, 1, -1)],
    [(0, -1, -1), (0, 2, 1), (1, -1, -1), (1, 1, 2)],
    [(0, 2, -1), (0, 1, 1), (1, -1, 2), (1, 1, 1)],
    [(0, 0, 2), (0, -1, 2), (1, 2, 0), (1, 2, -1)],
    [(0, 1, 2), (0, 2, 2), (1, 2, 1), (1, 2, 2)],
]
TICKS = [
    [(0, 1, 0), (0, -1, 0), (1, 0, 1), (1, 0, -1)],
    [(0, -1, 0), (0, 2, 0), (1, 0, -1), (1, 0, 2)],
    [(0, 2, 0), (0, 1, 0), (1, 0, 2), (1, 0, 1)],
    [(0, 0, -1), (0, -1, 1), (1, -1, 0), (1, 1, -1)],
    [(0, 1, -1), (0, 2, 1), (1, -1, 1), (1, 1, 2)],
]


def kernel(
    q_hbm, k_hbm, v_hbm, pk_hbm, pv_hbm, w_hbm, og_hbm, len_ref, freq_ref,
    out_ref, kg_out, vg_out,
    wall, og, part, rbuf, zbuf, early, kg, vg, gsend, grecv, acc, attn, qrot, prob_t, qin, kin, kall, vall, cos_t, sin_t, start_t,
    in_sem, wsend, wrecv, csend, crecv, zsend, zrecv, gssem, grsem,
):
    tok = q_hbm.shape[0]
    heads = q_hbm.shape[1] // HD
    prompt = pk_hbm.shape[0]
    n_tiles = tok // TILE
    scale = HD ** -0.5
    dp = lax.axis_index("dp")
    mp = lax.axis_index("mp")
    x0, y0, zl = dp % 4, (dp // 4) % 4, dp // 16
    zh, core = mp // 2, mp % 2

    def dpid(x, y, z):
        return z * 16 + y * 4 + x

    def pa(d):
        x = jnp.where(zl == 0, (x0 + d) % 4, x0)
        y = jnp.where(zl == 0, y0, (y0 + d) % 4)
        return (dpid(x, y, zl), mp)

    def pb(d):
        x = jnp.where(zl == 0, x0, (x0 + d) % 4)
        y = jnp.where(zl == 0, (y0 + d) % 4, y0)
        return (dpid(x, y, zl), mp)

    def slot(kind, da, db):
        x = (x0 + jnp.where(zl == 0, da, db) + 4) % 4
        y = (y0 + jnp.where(zl == 0, db, da) + 4) % 4
        t = jnp.where(kind == 0, zl, 1 - zl)
        return t * 16 + y * 4 + x

    a_up, a_dn, b_up, b_dn = pa(1), pa(3), pb(1), pb(3)
    z_peer = (dpid(x0, y0, 1 - zl), mp)
    c_peer = (dp, zh * 2 + 1 - core)
    far_peer = (dp, (1 - zh) * 2 + core)

    barrier = pltpu.get_barrier_semaphore()
    for peer in (a_up, a_dn, b_up, b_dn, z_peer, c_peer, far_peer):
        pl.semaphore_signal(barrier, inc=1, device_id=peer, device_id_type=MESH)

    me = slot(0, 0, 0)
    q_copy = pltpu.make_async_copy(q_hbm, qin, in_sem.at[0])
    k_copy = pltpu.make_async_copy(k_hbm, kin, in_sem.at[1])
    pk_copy = pltpu.make_async_copy(pk_hbm, kall.at[pl.ds(0, prompt)], in_sem.at[2])
    pv_copy = pltpu.make_async_copy(pv_hbm, vall.at[pl.ds(0, prompt)], in_sem.at[3])
    v_copy = pltpu.make_async_copy(v_hbm, vall.at[pl.ds(prompt, tok)], in_sem.at[4])
    w_copy = pltpu.make_async_copy(w_hbm, wall.at[me], in_sem.at[5])
    og_copy = pltpu.make_async_copy(og_hbm, og, in_sem.at[6])
    w_copy.start()
    for c in (k_copy, pk_copy, q_copy, pv_copy, v_copy):
        c.start()

    def rows(h):
        return pl.ds(h * HALF, HALF)

    def piece(s, h):
        return wall.at[s, rows(h)]

    def send_own(h, peer, n):
        pltpu.make_async_remote_copy(
            src_ref=w_hbm.at[rows(h)], dst_ref=piece(me, h), send_sem=wsend.at[n], recv_sem=wrecv.at[me, h],
            device_id=peer, device_id_type=MESH,
        ).start()

    def send(s, h, peer, n):
        pltpu.make_async_remote_copy(
            src_ref=piece(s, h), dst_ref=piece(s, h), send_sem=wsend.at[n], recv_sem=wrecv.at[s, h],
            device_id=peer, device_id_type=MESH,
        ).start()

    def arrived(s, h):
        pltpu.make_async_remote_copy(
            src_ref=piece(s, h), dst_ref=piece(s, h), send_sem=wsend.at[0], recv_sem=wrecv.at[s, h],
            device_id=z_peer, device_id_type=MESH,
        ).wait_recv()

    pl.semaphore_wait(barrier, 7)
    send_own(0, z_peer, 0)
    send_own(0, a_up, 1)
    send_own(1, a_dn, 2)
    send_own(0, b_up, 3)
    send_own(1, b_dn, 4)
    send_own(1, z_peer, 5)
    send_own(1, a_up, 6)
    send_own(0, a_dn, 7)
    send_own(1, b_up, 8)
    send_own(0, b_dn, 9)
    og_copy.start()

    t_col = lax.broadcasted_iota(jnp.int32, (tok, HD), 0)
    begin = jnp.zeros((tok, HD), jnp.int32)
    at = jnp.int32(0)
    for d in range(len_ref.shape[1]):
        begin = jnp.where(t_col >= at, at, begin)
        at = at + len_ref[0, d]
    start_t[...] = begin
    angle = (t_col - begin).astype(F32) * freq_ref[0:1, :]
    cos_t[...] = jnp.cos(angle)
    sin_t[...] = jnp.sin(angle) * freq_ref[1:2, :]

    def rotated(field, lo, n):
        f = field.astype(F32)
        return (f * cos_t[pl.ds(lo, n), :] + pltpu.roll(f, HD // 2, 1) * sin_t[pl.ds(lo, n), :]).astype(BF16)

    k_copy.wait()
    kall[pl.ds(prompt, tok), :] = rotated(kin[...], 0, tok)
    for c in (pk_copy, q_copy, pv_copy, v_copy, w_copy):
        c.wait()
    acc[...] = jnp.zeros_like(acc)

    def attention(i):
        lo = max(0, i - (DOC_MOST + TILE - 2) // TILE) * TILE
        n = (i + 1) * TILE - lo
        r = pl.ds(i * TILE, TILE)
        nt = (((1,), (1,)), ((), ()))

        def head(h, carry):
            lanes = pl.ds(pl.multiple_of(h * HD, HD), HD)
            q = rotated(qin[r, lanes], i * TILE, TILE)
            qrot[r, lanes] = q
            s_p = lax.dot_general(q, kall[pl.ds(0, prompt), :], nt, preferred_element_type=F32)
            s_t = lax.dot_general(q, kall[pl.ds(prompt + lo, n), :], nt, preferred_element_type=F32)
            col = lax.broadcasted_iota(jnp.int32, (TILE, n), 1) + lo
            row = lax.broadcasted_iota(jnp.int32, (TILE, n), 0) + i * TILE
            seen = (col <= row) & (col >= start_t[r, 0:1])
            s_t = jnp.where(seen, s_t, -1e30)
            top = jnp.maximum(jnp.max(s_p, axis=1, keepdims=True), jnp.max(s_t, axis=1, keepdims=True))
            e_p = jnp.exp((s_p - top) * scale)
            e_t = jnp.exp((s_t - top) * scale)
            inv = 1.0 / (jnp.sum(e_p, axis=1, keepdims=True) + jnp.sum(e_t, axis=1, keepdims=True))
            o = jnp.dot(e_p.astype(BF16), vall[pl.ds(0, prompt), :], preferred_element_type=F32)
            o = o + jnp.dot(e_t.astype(BF16), vall[pl.ds(prompt + lo, n), :], preferred_element_type=F32)
            attn[r, lanes] = (o * inv).astype(BF16)
            prob_t[lanes, r] = jnp.transpose(e_p * inv).astype(BF16)
            return carry

        lax.fori_loop(0, heads, head, 0, unroll=2)

    attention(0)
    attention(1)
    attention(2)

    arrived(slot(0, -1, 0), 0)
    send(slot(0, -1, 0), 0, a_up, 10)
    arrived(slot(0, 1, 0), 1)
    send(slot(0, 1, 0), 1, a_dn, 11)
    other = slot(1, 0, 0)
    arrived(other, 0)
    send(other, 0, b_up, 12)
    arrived(other, 1)
    send(other, 1, b_dn, 13)
    send(other, 1, b_up, 14)
    send(other, 0, b_dn, 15)
    send(other, 0, a_up, 16)
    send(other, 1, a_dn, 17)
    send(other, 1, a_up, 18)
    send(other, 0, a_dn, 19)
    attention(3)
    attention(4)
    arrived(slot(1, 0, -1), 0)
    send(slot(1, 0, -1), 0, b_up, 20)
    arrived(slot(1, 0, 1), 1)
    send(slot(1, 0, 1), 1, b_dn, 21)
    og_copy.wait()

    def slot_of(step, table, j):
        kind = 0 if j < 2 else 1
        return slot(kind, pick(step, [t[j][1] for t in table]), pick(step, [t[j][2] for t in table]))

    def tick(t):
        n = 22 + 8 * t
        up, dn = slot_of(t, TICKS, 0), slot_of(t, TICKS, 1)
        up2, dn2 = slot_of(t, TICKS, 2), slot_of(t, TICKS, 3)
        for h in range(2):
            send(up, h, b_up, n + h)
            send(dn, h, b_dn, n + 2 + h)
            send(up2, h, a_up, n + 4 + h)
            send(dn2, h, a_dn, n + 6 + h)

    def unit(step, j):
        i = step * 4 + jnp.where((step >= 3) & (zl == zh), (j + 2) % 4, j)
        flat = [u for four in STEPS for u in four]
        return slot(pick(i, [u[0] for u in flat]), pick(i, [u[1] for u in flat]), pick(i, [u[2] for u in flat]))

    def index_of(s):
        return (s // 16) * 8 + ((s // 4) % 2) * 4 + s % 4

    def core_copy(s):
        n = index_of(s)
        return pltpu.make_async_remote_copy(
            src_ref=part.at[s], dst_ref=rbuf.at[n], send_sem=csend.at[n], recv_sem=crecv.at[n],
            device_id=c_peer, device_id_type=MESH,
        )

    def far_copy(s):
        n = index_of(s) % 8
        return pltpu.make_async_remote_copy(
            src_ref=part.at[s], dst_ref=zbuf.at[n], send_sem=zsend.at[n], recv_sem=zrecv.at[n],
            device_id=far_peer, device_id_type=MESH,
        )

    def columns(n):
        return pl.ds(pl.multiple_of(n * UNIT, UNIT), UNIT)

    def hand_over(s):
        @pl.when((s // 8) % 2 != core)
        def _():
            core_copy(s).start()

    def add_grad(s, half):
        g = og[:, columns(s)]
        for b in range(half * HALF // UNIT, (half + 1) * HALF // UNIT):
            w = wall[s, b * UNIT:(b + 1) * UNIT, :]
            acc[:, b * UNIT:(b + 1) * UNIT] += lax.dot_general(
                g, w, (((1,), (1,)), ((), ())), preferred_element_type=F32
            )

    def process(s):
        part[s] = jnp.dot(attn[...], wall[s], preferred_element_type=F32).astype(BF16)
        hand_over(s)
        add_grad(s, 0)
        add_grad(s, 1)

    def combine(s):
        @pl.when((s // 8) % 2 == core)
        def _():
            n = index_of(s)
            core_copy(s).wait_recv()
            part[s] = (part[s].astype(F32) + rbuf[n].astype(F32)).astype(BF16)

            @pl.when(s // 16 != zh)
            def _():
                far_copy(s).start()

    def both(s):
        arrived(s, 0)
        arrived(s, 1)

    def step_body(step, carry):
        @pl.when(step == 0)
        def _():
            arrived(slot(0, -1, 0), 1)
            arrived(slot(0, 1, 0), 0)

        @pl.when(step == 1)
        def _():
            both(slot(0, 0, 1))
            both(slot(0, 0, -1))
            both(slot(0, 2, 0))
            arrived(slot(1, 0, -1), 1)
            arrived(slot(1, 0, 1), 0)
            tick(0)

        @pl.when(step == 2)
        def _():
            both(slot(1, 1, 0))
            both(slot(1, -1, 0))
            both(slot(1, 0, 2))
            tick(1)

        @pl.when((step >= 3) & (step <= 5))
        def _():
            for j in range(4):
                both(unit(step, j))
            tick(step - 1)

        def one(j, c):
            s = unit(step, j)

            @pl.when(step == 6)
            def _():
                both(s)

            process(s)

            @pl.when(j > 0)
            def _():
                combine(unit(step, j - 1))

            return c

        lax.fori_loop(0, 4, one, 0)
        combine(unit(step, 3))
        return carry

    lax.fori_loop(0, 7, step_body, 0)

    nn = (((1,), (0,)), ((), ()))
    nt = (((1,), (1,)), ((), ()))
    kg[...] = jnp.zeros_like(kg)
    vg[...] = jnp.zeros_like(vg)

    def grads(h, c):
        lanes = pl.ds(pl.multiple_of(h * HD, HD), HD)
        g32 = acc[:, lanes].astype(BF16).astype(F32)
        g = g32.astype(BF16)
        p = prob_t[lanes, :]
        weighed = (g32 * attn[:, lanes].astype(F32)).astype(BF16)
        delta = lax.dot_general(jnp.ones((8, HD), BF16), weighed, nt, preferred_element_type=F32)[0:1, :]
        gp = lax.dot_general(vall[pl.ds(0, prompt), :], g, nt, preferred_element_type=F32)
        ds = (p.astype(F32) * (gp - delta) * scale).astype(BF16)
        kg[...] += lax.dot_general(ds, qrot[:, lanes], nn, preferred_element_type=F32)
        vg[...] += lax.dot_general(p, g, nn, preferred_element_type=F32)
        return c

    def first_half(j, c):
        s = unit(7, j)
        arrived(s, 0)
        early[j] = jnp.dot(attn[:, 0:HALF], wall[s, 0:HALF, :], preferred_element_type=F32)
        add_grad(s, 0)
        return c

    lax.fori_loop(0, 4, first_half, 0)
    lax.fori_loop(0, heads // 2, grads, 0)

    def second_product(j, c):
        s = unit(7, j)
        rest = jnp.dot(attn[:, HALF:2 * HALF], wall[s, HALF:2 * HALF, :], preferred_element_type=F32)
        part[s] = (early[j] + rest).astype(BF16)
        hand_over(s)
        return c

    def leaving(j, c):
        arrived(unit(7, j), 1)
        return second_product(j, c)

    lax.fori_loop(0, 2, leaving, 0)

    def second_grad(j, c):
        @pl.when(j >= 2)
        def _():
            arrived(unit(7, j), 1)

        add_grad(unit(7, j), 1)

        @pl.when(j >= 2)
        def _():
            combine(unit(7, j - 2))

        return c

    lax.fori_loop(0, 4, second_grad, 0)
    lax.fori_loop(heads // 2, heads, grads, 0)

    n_dp = gsend.shape[0]
    own_rows = prompt // n_dp
    gsend[:, 0:own_rows, :] = kg[...].reshape(n_dp, own_rows, HD)
    gsend[:, own_rows:2 * own_rows, :] = vg[...].reshape(n_dp, own_rows, HD)

    def grad_send(j, c):
        pltpu.make_async_remote_copy(
            src_ref=gsend.at[(dp + j) % n_dp], dst_ref=grecv.at[dp], send_sem=gssem, recv_sem=grsem,
            device_id=((dp + j) % n_dp, mp), device_id_type=MESH,
        ).start()
        return c

    lax.fori_loop(1, n_dp, grad_send, 0)
    grecv[dp] = gsend[dp]
    lax.fori_loop(2, 4, second_product, 0)

    def finish(i, c):
        s = unit(i // 4, i % 4)

        @pl.when(((s // 8) % 2 == core) & (s // 16 == zh))
        def _():
            n = index_of(s) % 8
            far_copy(s).wait_recv()
            out_ref[:, columns(n)] = (part[s].astype(F32) + zbuf[n].astype(F32)).astype(BF16)

        return c

    lax.fori_loop(0, 28, finish, 0)
    combine(unit(7, 2))
    combine(unit(7, 3))

    def drain(n, c):
        pltpu.make_async_remote_copy(
            src_ref=piece(0, 0), dst_ref=piece(0, 0), send_sem=wsend.at[n], recv_sem=wrecv.at[0, 0],
            device_id=z_peer, device_id_type=MESH,
        ).wait_send()
        return c

    lax.fori_loop(0, 62, drain, 0)

    def drain_parts(s, c):
        @pl.when((s // 8) % 2 != core)
        def _():
            core_copy(s).wait_send()

        @pl.when(((s // 8) % 2 == core) & (s // 16 != zh))
        def _():
            far_copy(s).wait_send()

        return c

    lax.fori_loop(0, n_dp, drain_parts, 0)
    everyone = pltpu.make_async_remote_copy(
        src_ref=gsend.at[pl.ds(0, n_dp - 1)], dst_ref=grecv.at[pl.ds(0, n_dp - 1)], send_sem=gssem, recv_sem=grsem,
        device_id=z_peer, device_id_type=MESH,
    )
    everyone.wait_recv()
    total = jnp.sum(grecv[...], axis=0)
    kg_out[...] = total[0:own_rows, :]
    vg_out[...] = total[own_rows:2 * own_rows, :]
    everyone.wait_send()
    lax.fori_loop(28, 32, finish, 0)


def per_device(queries, keys, values, prompt_keys, prompt_values, out_weight, out_grad, lengths):
    tok, width = queries.shape
    prompt = prompt_keys.shape[0]
    n_dp = lax.axis_size("dp")
    own_rows = prompt // n_dp
    half = HD // 2
    freq = ROPE_BASE ** (-2.0 * np.arange(half) / HD)
    table = np.zeros((8, HD), np.float32)
    table[0] = np.concatenate([freq, freq])
    table[1] = np.concatenate([-np.ones(half), np.ones(half)])
    anywhere = pl.BlockSpec(memory_space=pl.ANY)
    vmem = pl.BlockSpec(memory_space=pltpu.VMEM)
    dma = pltpu.SemaphoreType.DMA
    return pl.pallas_call(
        kernel,
        out_shape=(
            pltpu.VMEM((tok, 8 * UNIT), BF16),
            pltpu.VMEM((own_rows, HD), F32),
            pltpu.VMEM((own_rows, HD), F32),
        ),
        in_specs=[anywhere] * 7 + [pl.BlockSpec(memory_space=pltpu.SMEM), vmem],
        out_specs=(vmem, vmem, vmem),
        scratch_shapes=[
            pltpu.VMEM((n_dp, width, UNIT), BF16),
            pltpu.VMEM((tok, n_dp * UNIT), BF16),
            pltpu.VMEM((n_dp, tok, UNIT), BF16),
            pltpu.VMEM((16, tok, UNIT), BF16),
            pltpu.VMEM((8, tok, UNIT), BF16),
            pltpu.VMEM((4, tok, UNIT), F32),
            pltpu.VMEM((prompt, HD), F32),
            pltpu.VMEM((prompt, HD), F32),
            pltpu.VMEM((n_dp, 2 * own_rows, HD), F32),
            pltpu.VMEM((n_dp, 2 * own_rows, HD), F32),
            pltpu.VMEM((tok, width), F32),
            pltpu.VMEM((tok, width), BF16),
            pltpu.VMEM((tok, width), BF16),
            pltpu.VMEM((width, tok), BF16),
            pltpu.VMEM((tok, width), BF16),
            pltpu.VMEM((tok, HD), BF16),
            pltpu.VMEM((prompt + tok, HD), BF16),
            pltpu.VMEM((prompt + tok, HD), BF16),
            pltpu.VMEM((tok, HD), F32),
            pltpu.VMEM((tok, HD), F32),
            pltpu.VMEM((tok, HD), jnp.int32),
            dma((7,)),
            dma((62,)),
            dma((n_dp, 2)),
            dma((16,)),
            dma((16,)),
            dma((8,)),
            dma((8,)),
            dma,
            dma,
        ],
        compiler_params=pltpu.CompilerParams(
            collective_id=0, has_side_effects=True, vmem_limit_bytes=58 * 1024 * 1024
        ),
    )(queries, keys, values, prompt_keys, prompt_values, out_weight, out_grad, lengths, jnp.asarray(table))


def solution(mesh):
    in_specs = (
        P("dp", "mp"),
        P("dp", "mp"),
        P("dp", "mp"),
        P(None, "mp"),
        P(None, "mp"),
        P("mp", "dp"),
        P("dp", None),
        P("dp", None),
    )
    out_specs = (P("dp", "mp"), P("dp", "mp"), P("dp", "mp"))
    return jax.shard_map(
        per_device, mesh=mesh, in_specs=in_specs, out_specs=out_specs, check_vma=False
    )
```

```python
import functools
import math

import jax
import jax.numpy as jnp
import numpy as np
from jax import lax
from jax.experimental import pallas as pl
from jax.experimental.pallas import tpu as pltpu
from jax.sharding import PartitionSpec as P

HD = 128
DOC_MOST = 320
ROPE_BASE = 1000000.0
TILE = 128
HALF = 512
UNIT = 256
MESH = pl.DeviceIdType.MESH
F32 = jnp.float32
BF16 = jnp.bfloat16


def pick(i, values):
    out = values[0]
    for k in range(1, len(values)):
        out = jnp.where(i == k, values[k], out)
    return out


STEPS = [
    [(0, 0, 0), (0, 1, 0), (0, -1, 0), (1, 0, 0)],
    [(0, 0, 1), (0, 0, -1), (0, 2, 0), (1, 0, 1)],
    [(1, 0, -1), (1, 1, 0), (1, -1, 0), (0, 1, -1)],
    [(0, -1, 1), (1, 0, 2), (1, -1, 1), (1, 1, -1)],
    [(0, -1, -1), (0, 2, 1), (1, -1, -1), (1, 1, 1)],
    [(0, 2, -1), (0, 1, 1), (1, -1, 2), (1, 1, 2)],
    [(0, 0, 2), (0, -1, 2), (1, 2, 0), (1, 2, -1)],
    [(0, 1, 2), (0, 2, 2), (1, 2, 1), (1, 2, 2)],
]
TICKS = [
    [(0, 1, 0), (0, -1, 0), (1, 0, 1), (1, 0, -1)],
    [(0, -1, 0), (0, 2, 0), (1, 0, -1), (1, 0, 1)],
    [(0, 2, 0), (0, 1, 0), (1, 0, 2), (1, 0, 2)],
    [(0, 0, -1), (0, -1, 1), (1, -1, 0), (1, 1, -1)],
    [(0, 1, -1), (0, 2, 1), (1, -1, 1), (1, 1, 2)],
]


def kernel(
    q_hbm, k_hbm, v_hbm, pk_hbm, pv_hbm, w_hbm, og_hbm, len_ref, freq_ref,
    out_ref, kg_out, vg_out,
    wall, og, part, rbuf, zbuf, early, kg, vg, gsend, grecv, acc, attn, qrot, prob_t, qin, kin, kall, vall, cos_t, sin_t, start_t,
    in_sem, wsend, wrecv, csend, crecv, zsend, zrecv, gssem, grsem,
):
    tok = q_hbm.shape[0]
    heads = q_hbm.shape[1] // HD
    prompt = pk_hbm.shape[0]
    n_tiles = tok // TILE
    scale = HD ** -0.5
    dp = lax.axis_index("dp")
    mp = lax.axis_index("mp")
    x0, y0, zl = dp % 4, (dp // 4) % 4, dp // 16
    zh, core = mp // 2, mp % 2

    def dpid(x, y, z):
        return z * 16 + y * 4 + x

    def pa(d):
        x = jnp.where(zl == 0, (x0 + d) % 4, x0)
        y = jnp.where(zl == 0, y0, (y0 + d) % 4)
        return (dpid(x, y, zl), mp)

    def pb(d):
        x = jnp.where(zl == 0, x0, (x0 + d) % 4)
        y = jnp.where(zl == 0, (y0 + d) % 4, y0)
        return (dpid(x, y, zl), mp)

    def slot(kind, da, db):
        x = (x0 + jnp.where(zl == 0, da, db) + 4) % 4
        y = (y0 + jnp.where(zl == 0, db, da) + 4) % 4
        t = jnp.where(kind == 0, zl, 1 - zl)
        return t * 16 + y * 4 + x

    a_up, a_dn, b_up, b_dn = pa(1), pa(3), pb(1), pb(3)
    z_peer = (dpid(x0, y0, 1 - zl), mp)
    c_peer = (dp, zh * 2 + 1 - core)
    far_peer = (dp, (1 - zh) * 2 + core)

    barrier = pltpu.get_barrier_semaphore()
    for peer in (a_up, a_dn, b_up, b_dn, z_peer, c_peer, far_peer):
        pl.semaphore_signal(barrier, inc=1, device_id=peer, device_id_type=MESH)

    me = slot(0, 0, 0)
    q_copy = pltpu.make_async_copy(q_hbm, qin, in_sem.at[0])
    k_copy = pltpu.make_async_copy(k_hbm, kin, in_sem.at[1])
    pk_copy = pltpu.make_async_copy(pk_hbm, kall.at[pl.ds(0, prompt)], in_sem.at[2])
    pv_copy = pltpu.make_async_copy(pv_hbm, vall.at[pl.ds(0, prompt)], in_sem.at[3])
    v_copy = pltpu.make_async_copy(v_hbm, vall.at[pl.ds(prompt, tok)], in_sem.at[4])
    w_copy = pltpu.make_async_copy(w_hbm, wall.at[me], in_sem.at[5])
    og_copy = pltpu.make_async_copy(og_hbm, og, in_sem.at[6])
    w_copy.start()
    for c in (k_copy, pk_copy, q_copy, pv_copy, v_copy):
        c.start()

    def rows(h):
        return pl.ds(h * HALF, HALF)

    def piece(s, h):
        return wall.at[s, rows(h)]

    def send_own(h, peer):
        pltpu.make_async_remote_copy(
            src_ref=w_hbm.at[rows(h)], dst_ref=piece(me, h), send_sem=wsend, recv_sem=wrecv.at[me, h],
            device_id=peer, device_id_type=MESH,
        ).start()

    def send(s, h, peer):
        pltpu.make_async_remote_copy(
            src_ref=piece(s, h), dst_ref=piece(s, h), send_sem=wsend, recv_sem=wrecv.at[s, h],
            device_id=peer, device_id_type=MESH,
        ).start()

    def arrived(s, h):
        pltpu.make_async_remote_copy(
            src_ref=piece(s, h), dst_ref=piece(s, h), send_sem=wsend, recv_sem=wrecv.at[s, h],
            device_id=z_peer, device_id_type=MESH,
        ).wait_recv()

    pl.semaphore_wait(barrier, 7)
    send_own(0, z_peer)
    send_own(0, a_up)
    send_own(1, a_dn)
    send_own(0, b_up)
    send_own(1, b_dn)
    send_own(1, z_peer)
    send_own(1, a_up)
    send_own(0, a_dn)
    send_own(1, b_up)
    send_own(0, b_dn)
    og_copy.start()

    t_col = lax.broadcasted_iota(jnp.int32, (tok, HD), 0)
    begin = jnp.zeros((tok, HD), jnp.int32)
    at = jnp.int32(0)
    for d in range(len_ref.shape[1]):
        begin = jnp.where(t_col >= at, at, begin)
        at = at + len_ref[0, d]
    start_t[...] = begin
    angle = (t_col - begin).astype(F32) * freq_ref[0:1, :]
    cos_t[...] = jnp.cos(angle)
    sin_t[...] = jnp.sin(angle) * freq_ref[1:2, :]

    def rotated(field, lo, n):
        f = field.astype(F32)
        return (f * cos_t[pl.ds(lo, n), :] + pltpu.roll(f, HD // 2, 1) * sin_t[pl.ds(lo, n), :]).astype(BF16)

    k_copy.wait()
    kall[pl.ds(prompt, tok), :] = rotated(kin[...], 0, tok)
    for c in (pk_copy, q_copy, pv_copy, v_copy, w_copy):
        c.wait()
    acc[...] = jnp.zeros_like(acc)

    def attention(i):
        lo = max(0, i - (DOC_MOST + TILE - 2) // TILE) * TILE
        n = (i + 1) * TILE - lo
        r = pl.ds(i * TILE, TILE)
        nt = (((1,), (1,)), ((), ()))

        def head(h, carry):
            lanes = pl.ds(pl.multiple_of(h * HD, HD), HD)
            q = rotated(qin[r, lanes], i * TILE, TILE)
            qrot[r, lanes] = q
            s_p = lax.dot_general(q, kall[pl.ds(0, prompt), :], nt, preferred_element_type=F32)
            s_t = lax.dot_general(q, kall[pl.ds(prompt + lo, n), :], nt, preferred_element_type=F32)
            col = lax.broadcasted_iota(jnp.int32, (TILE, n), 1) + lo
            row = lax.broadcasted_iota(jnp.int32, (TILE, n), 0) + i * TILE
            seen = (col <= row) & (col >= start_t[r, 0:1])
            s_t = jnp.where(seen, s_t, -1e30)
            top = jnp.maximum(jnp.max(s_p, axis=1, keepdims=True), jnp.max(s_t, axis=1, keepdims=True))
            e_p = jnp.exp((s_p - top) * scale)
            e_t = jnp.exp((s_t - top) * scale)
            inv = 1.0 / (jnp.sum(e_p, axis=1, keepdims=True) + jnp.sum(e_t, axis=1, keepdims=True))
            o = jnp.dot(e_p.astype(BF16), vall[pl.ds(0, prompt), :], preferred_element_type=F32)
            o = o + jnp.dot(e_t.astype(BF16), vall[pl.ds(prompt + lo, n), :], preferred_element_type=F32)
            attn[r, lanes] = (o * inv).astype(BF16)
            prob_t[lanes, r] = jnp.transpose(e_p * inv).astype(BF16)
            return carry

        lax.fori_loop(0, heads, head, 0, unroll=2)

    def both(s):
        arrived(s, 0)
        arrived(s, 1)

    attention(0)
    attention(1)
    arrived(slot(0, -1, 0), 0)
    send(slot(0, -1, 0), 0, a_up)
    arrived(slot(0, 1, 0), 1)
    send(slot(0, 1, 0), 1, a_dn)
    other = slot(1, 0, 0)
    for h in range(2):
        arrived(other, h)
        send(other, h, b_up)
        send(other, h, b_dn)
        send(other, h, a_up)
        send(other, h, a_dn)
        attention(2 + h)
    arrived(slot(0, -1, 0), 1)
    arrived(slot(0, 1, 0), 0)
    for h in range(2):
        send(slot(0, 1, 0), h, b_up)
        send(slot(0, -1, 0), h, b_dn)
    attention(4)
    both(slot(1, 0, -1))
    both(slot(1, 0, 1))
    send(slot(1, 0, -1), 0, b_up)
    send(slot(1, 0, 1), 1, b_dn)
    for h in range(2):
        send(slot(1, 0, 1), h, a_up)
        send(slot(1, 0, -1), h, a_dn)
    og_copy.wait()

    def slot_of(step, table, j):
        kind = 0 if j < 2 else 1
        return slot(kind, pick(step, [t[j][1] for t in table]), pick(step, [t[j][2] for t in table]))

    def tick(t):
        up, dn = slot_of(t, TICKS, 0), slot_of(t, TICKS, 1)
        up2, dn2 = slot_of(t, TICKS, 2), slot_of(t, TICKS, 3)
        for h in range(2):
            send(up, h, b_up)
            send(dn, h, b_dn)
            send(up2, h, a_up)
            send(dn2, h, a_dn)

    def unit(step, j):
        i = step * 4 + jnp.where((step >= 4) & (zl == zh), (j + 2) % 4, j)
        flat = [u for four in STEPS for u in four]
        return slot(pick(i, [u[0] for u in flat]), pick(i, [u[1] for u in flat]), pick(i, [u[2] for u in flat]))

    def index_of(s):
        return (s // 16) * 8 + ((s // 4) % 2) * 4 + s % 4

    def core_copy(s):
        n = index_of(s)
        return pltpu.make_async_remote_copy(
            src_ref=part.at[s], dst_ref=rbuf.at[n], send_sem=csend, recv_sem=crecv.at[n],
            device_id=c_peer, device_id_type=MESH,
        )

    def far_copy(s):
        n = index_of(s) % 8
        return pltpu.make_async_remote_copy(
            src_ref=part.at[s], dst_ref=zbuf.at[n], send_sem=zsend, recv_sem=zrecv.at[n],
            device_id=far_peer, device_id_type=MESH,
        )

    def columns(n):
        return pl.ds(pl.multiple_of(n * UNIT, UNIT), UNIT)

    def hand_over(s):
        @pl.when((s // 8) % 2 != core)
        def _():
            core_copy(s).start()

    def add_grads(step, lo, hi):
        four = [unit(step, j) for j in range(4)]
        g = jnp.concatenate([og[:, columns(s)] for s in four], axis=1)
        for b in range(lo // UNIT, hi // UNIT):
            w = jnp.concatenate([wall[s, b * UNIT:(b + 1) * UNIT, :] for s in four], axis=1)
            acc[:, b * UNIT:(b + 1) * UNIT] += lax.dot_general(
                g, w, (((1,), (1,)), ((), ())), preferred_element_type=F32
            )

    def process(s):
        part[s] = jnp.dot(attn[...], wall[s], preferred_element_type=F32).astype(BF16)
        hand_over(s)

    def combine(s):
        @pl.when((s // 8) % 2 == core)
        def _():
            n = index_of(s)
            core_copy(s).wait_recv()
            part[s] = (part[s].astype(F32) + rbuf[n].astype(F32)).astype(BF16)

            @pl.when(s // 16 != zh)
            def _():
                far_copy(s).start()

    def finish(i, c):
        s = unit(i // 4, i % 4)

        @pl.when(((s // 8) % 2 == core) & (s // 16 == zh))
        def _():
            n = index_of(s) % 8
            far_copy(s).wait_recv()
            out_ref[:, columns(n)] = (part[s].astype(F32) + zbuf[n].astype(F32)).astype(BF16)

        return c

    def step_body(step, carry):
        @pl.when(step == 1)
        def _():
            both(slot(0, 0, 1))
            both(slot(0, 0, -1))
            both(slot(0, 2, 0))
            tick(1)

        @pl.when(step == 2)
        def _():
            both(slot(1, 1, 0))
            both(slot(1, -1, 0))
            both(slot(0, 1, -1))

        @pl.when((step >= 3) & (step <= 5))
        def _():
            for j in range(4):
                both(unit(step, j))
            tick(step - 1)

        def one(j, c):
            s = unit(step, j)

            @pl.when(step == 6)
            def _():
                both(s)

            process(s)

            @pl.when(j > 0)
            def _():
                combine(unit(step, j - 1))

            return c

        lax.fori_loop(0, 4, one, 0)
        add_grads(step, 0, acc.shape[1])
        combine(unit(step, 3))

        @pl.when(step >= 2)
        def _():
            lax.fori_loop(4 * (step - 2), 4 * (step - 1), finish, 0)

        return carry

    lax.fori_loop(0, 7, step_body, 0)

    nn = (((1,), (0,)), ((), ()))
    nt = (((1,), (1,)), ((), ()))
    kg[...] = jnp.zeros_like(kg)
    vg[...] = jnp.zeros_like(vg)

    def grads(h, c):
        lanes = pl.ds(pl.multiple_of(h * HD, HD), HD)
        g32 = acc[:, lanes].astype(BF16).astype(F32)
        g = g32.astype(BF16)
        p = prob_t[lanes, :]
        weighed = (g32 * attn[:, lanes].astype(F32)).astype(BF16)
        delta = lax.dot_general(jnp.ones((8, HD), BF16), weighed, nt, preferred_element_type=F32)[0:1, :]
        gp = lax.dot_general(vall[pl.ds(0, prompt), :], g, nt, preferred_element_type=F32)
        ds = (p.astype(F32) * (gp - delta) * scale).astype(BF16)
        kg[...] += lax.dot_general(ds, qrot[:, lanes], nn, preferred_element_type=F32)
        vg[...] += lax.dot_general(p, g, nn, preferred_element_type=F32)
        return c

    def first_half(j, c):
        s = unit(7, j)
        arrived(s, 0)
        early[j] = jnp.dot(attn[:, 0:HALF], wall[s, 0:HALF, :], preferred_element_type=F32)
        return c

    lax.fori_loop(0, 4, first_half, 0)
    add_grads(7, 0, HALF)
    lax.fori_loop(0, heads // 2, grads, 0, unroll=4)

    lax.fori_loop(20, 24, finish, 0)

    def second_product(j, c):
        s = unit(7, j)
        rest = jnp.dot(attn[:, HALF:2 * HALF], wall[s, HALF:2 * HALF, :], preferred_element_type=F32)
        part[s] = (early[j] + rest).astype(BF16)
        hand_over(s)
        return c

    def leaving(j, c):
        arrived(unit(7, j), 1)
        return second_product(j, c)

    lax.fori_loop(0, 2, leaving, 0)

    arrived(unit(7, 2), 1)
    arrived(unit(7, 3), 1)
    add_grads(7, HALF, 2 * HALF)
    combine(unit(7, 0))
    combine(unit(7, 1))
    lax.fori_loop(heads // 2, heads, grads, 0, unroll=4)

    n_dp = gsend.shape[0]
    own_rows = prompt // n_dp
    gsend[:, 0:own_rows, :] = kg[...].reshape(n_dp, own_rows, HD)
    gsend[:, own_rows:2 * own_rows, :] = vg[...].reshape(n_dp, own_rows, HD)

    def grad_send(j, c):
        pltpu.make_async_remote_copy(
            src_ref=gsend.at[(dp + j) % n_dp], dst_ref=grecv.at[dp], send_sem=gssem, recv_sem=grsem,
            device_id=((dp + j) % n_dp, mp), device_id_type=MESH,
        ).start()
        return c

    lax.fori_loop(1, n_dp, grad_send, 0)
    grecv[dp] = gsend[dp]
    lax.fori_loop(2, 4, second_product, 0)

    lax.fori_loop(24, 28, finish, 0)
    combine(unit(7, 2))
    combine(unit(7, 3))

    everyone = pltpu.make_async_remote_copy(
        src_ref=gsend.at[pl.ds(0, n_dp - 1)], dst_ref=grecv.at[pl.ds(0, n_dp - 1)], send_sem=gssem, recv_sem=grsem,
        device_id=z_peer, device_id_type=MESH,
    )
    everyone.wait_recv()
    total = jnp.sum(grecv[...], axis=0)
    kg_out[...] = total[0:own_rows, :]
    vg_out[...] = total[own_rows:2 * own_rows, :]
    everyone.wait_send()
    lax.fori_loop(28, 32, finish, 0)
    for buf, sem in ((wall.at[pl.ds(0, n_dp - 1)], wsend), (rbuf, csend), (zbuf, zsend)):
        pltpu.make_async_remote_copy(
            src_ref=buf, dst_ref=buf, send_sem=sem, recv_sem=wrecv.at[0, 0], device_id=z_peer, device_id_type=MESH
        ).wait_send()


def write_out(*refs):
    n = len(refs) // 2
    copies = [pltpu.make_async_copy(refs[i], refs[n + i], refs[2 * n].at[i]) for i in range(n)]
    for c in copies:
        c.start()
    for c in copies:
        c.wait()


def per_device(queries, keys, values, prompt_keys, prompt_values, out_weight, out_grad, lengths):
    tok, width = queries.shape
    prompt = prompt_keys.shape[0]
    n_dp = lax.axis_size("dp")
    own_rows = prompt // n_dp
    half = HD // 2
    freq = ROPE_BASE ** (-2.0 * np.arange(half) / HD)
    table = np.zeros((8, HD), np.float32)
    table[0] = np.concatenate([freq, freq])
    table[1] = np.concatenate([-np.ones(half), np.ones(half)])
    anywhere = pl.BlockSpec(memory_space=pl.ANY)
    vmem = pl.BlockSpec(memory_space=pltpu.VMEM)
    dma = pltpu.SemaphoreType.DMA
    results = pl.pallas_call(
        kernel,
        out_shape=(
            pltpu.VMEM((tok, 8 * UNIT), BF16),
            pltpu.VMEM((own_rows, HD), F32),
            pltpu.VMEM((own_rows, HD), F32),
        ),
        in_specs=[anywhere] * 7 + [pl.BlockSpec(memory_space=pltpu.SMEM), vmem],
        out_specs=(vmem, vmem, vmem),
        scratch_shapes=[
            pltpu.VMEM((n_dp, width, UNIT), BF16),
            pltpu.VMEM((tok, n_dp * UNIT), BF16),
            pltpu.VMEM((n_dp, tok, UNIT), BF16),
            pltpu.VMEM((16, tok, UNIT), BF16),
            pltpu.VMEM((8, tok, UNIT), BF16),
            pltpu.VMEM((4, tok, UNIT), F32),
            pltpu.VMEM((prompt, HD), F32),
            pltpu.VMEM((prompt, HD), F32),
            pltpu.VMEM((n_dp, 2 * own_rows, HD), F32),
            pltpu.VMEM((n_dp, 2 * own_rows, HD), F32),
            pltpu.VMEM((tok, width), F32),
            pltpu.VMEM((tok, width), BF16),
            pltpu.VMEM((tok, width), BF16),
            pltpu.VMEM((width, tok), BF16),
            pltpu.VMEM((tok, width), BF16),
            pltpu.VMEM((tok, HD), BF16),
            pltpu.VMEM((prompt + tok, HD), BF16),
            pltpu.VMEM((prompt + tok, HD), BF16),
            pltpu.VMEM((tok, HD), F32),
            pltpu.VMEM((tok, HD), F32),
            pltpu.VMEM((tok, HD), jnp.int32),
            dma((7,)),
            dma,
            dma((n_dp, 2)),
            dma,
            dma((16,)),
            dma,
            dma((8,)),
            dma,
            dma,
        ],
        compiler_params=pltpu.CompilerParams(
            collective_id=0, has_side_effects=True, vmem_limit_bytes=60 * 1024 * 1024
        ),
    )(queries, keys, values, prompt_keys, prompt_values, out_weight, out_grad, lengths, jnp.asarray(table))
    return pl.pallas_call(
        write_out,
        out_shape=tuple(jax.ShapeDtypeStruct(r.shape, r.dtype) for r in results),
        in_specs=[vmem] * 3,
        out_specs=(anywhere,) * 3,
        scratch_shapes=[dma((3,))],
    )(*(pltpu.with_memory_space_constraint(r, pltpu.VMEM) for r in results))


def solution(mesh):
    in_specs = (
        P("dp", "mp"),
        P("dp", "mp"),
        P("dp", "mp"),
        P(None, "mp"),
        P(None, "mp"),
        P("mp", "dp"),
        P("dp", None),
        P("dp", None),
    )
    out_specs = (P("dp", "mp"), P("dp", "mp"), P("dp", "mp"))
    return jax.shard_map(
        per_device, mesh=mesh, in_specs=in_specs, out_specs=out_specs, check_vma=False
    )
```

```python
import functools
import math

import jax
import jax.numpy as jnp
import numpy as np
from jax import lax
from jax.experimental import pallas as pl
from jax.experimental.pallas import tpu as pltpu
from jax.sharding import PartitionSpec as P

HD = 128
DOC_MOST = 320
ROPE_BASE = 1000000.0
TILE = 128
HALF = 512
UNIT = 256
MESH = pl.DeviceIdType.MESH
F32 = jnp.float32
BF16 = jnp.bfloat16


def pick(i, values):
    out = values[0]
    for k in range(1, len(values)):
        out = jnp.where(i == k, values[k], out)
    return out


STEPS = [
    [(0, 0, 0), (0, 1, 0), (0, -1, 0), (1, 0, 0)],
    [(0, 0, 1), (0, 0, -1), (0, 2, 0), (1, 0, 1)],
    [(1, 0, -1), (1, 1, 0), (1, -1, 0), (0, 1, -1)],
    [(0, -1, 1), (1, 0, 2), (1, -1, 1), (1, 1, -1)],
    [(0, -1, -1), (0, 2, 1), (1, -1, -1), (1, 1, 1)],
    [(0, 2, -1), (0, 1, 1), (1, -1, 2), (1, 1, 2)],
    [(0, 0, 2), (0, -1, 2), (1, 2, 0), (1, 2, -1)],
    [(0, 1, 2), (0, 2, 2), (1, 2, 1), (1, 2, 2)],
]
TICKS = [
    [(0, 1, 0), (0, -1, 0), (1, 0, 1), (1, 0, -1)],
    [(0, -1, 0), (0, 2, 0), (1, 0, -1), (1, 0, 1)],
    [(0, 2, 0), (0, 1, 0), (1, 0, 2), (1, 0, 2)],
    [(0, 0, -1), (0, -1, 1), (1, -1, 0), (1, 1, -1)],
    [(0, 1, -1), (0, 2, 1), (1, -1, 1), (1, 1, 2)],
]


def kernel(
    q_hbm, k_hbm, v_hbm, pk_hbm, pv_hbm, w_hbm, og_hbm, len_ref, freq_ref,
    out_ref, kg_out, vg_out,
    wall, og, part, rbuf, zbuf, kg, vg, gsend, grecv, acc, attn, qrot, prob_t, qin, kin, kall, vall, cos_t, sin_t, start_t,
    in_sem, wsend, wrecv, csend, crecv, zsend, zrecv, gssem, grsem,
):
    tok = q_hbm.shape[0]
    heads = q_hbm.shape[1] // HD
    prompt = pk_hbm.shape[0]
    n_tiles = tok // TILE
    scale = HD ** -0.5
    dp = lax.axis_index("dp")
    mp = lax.axis_index("mp")
    x0, y0, zl = dp % 4, (dp // 4) % 4, dp // 16
    zh, core = mp // 2, mp % 2

    def dpid(x, y, z):
        return z * 16 + y * 4 + x

    def pa(d):
        x = jnp.where(zl == 0, (x0 + d) % 4, x0)
        y = jnp.where(zl == 0, y0, (y0 + d) % 4)
        return (dpid(x, y, zl), mp)

    def pb(d):
        x = jnp.where(zl == 0, x0, (x0 + d) % 4)
        y = jnp.where(zl == 0, (y0 + d) % 4, y0)
        return (dpid(x, y, zl), mp)

    def slot(kind, da, db):
        x = (x0 + jnp.where(zl == 0, da, db) + 4) % 4
        y = (y0 + jnp.where(zl == 0, db, da) + 4) % 4
        t = jnp.where(kind == 0, zl, 1 - zl)
        return t * 16 + y * 4 + x

    a_up, a_dn, b_up, b_dn = pa(1), pa(3), pb(1), pb(3)
    z_peer = (dpid(x0, y0, 1 - zl), mp)
    c_peer = (dp, zh * 2 + 1 - core)
    far_peer = (dp, (1 - zh) * 2 + core)

    barrier = pltpu.get_barrier_semaphore()
    for peer in (a_up, a_dn, b_up, b_dn, z_peer, c_peer, far_peer):
        pl.semaphore_signal(barrier, inc=1, device_id=peer, device_id_type=MESH)

    me = slot(0, 0, 0)
    q_copy = pltpu.make_async_copy(q_hbm, qin, in_sem.at[0])
    k_copy = pltpu.make_async_copy(k_hbm, kin, in_sem.at[1])
    pk_copy = pltpu.make_async_copy(pk_hbm, kall.at[pl.ds(0, prompt)], in_sem.at[2])
    pv_copy = pltpu.make_async_copy(pv_hbm, vall.at[pl.ds(0, prompt)], in_sem.at[3])
    v_copy = pltpu.make_async_copy(v_hbm, vall.at[pl.ds(prompt, tok)], in_sem.at[4])
    w_copy = pltpu.make_async_copy(w_hbm, wall.at[me], in_sem.at[5])
    og_copy = pltpu.make_async_copy(og_hbm, og, in_sem.at[6])
    w_copy.start()
    for c in (k_copy, pk_copy, q_copy, pv_copy, v_copy):
        c.start()

    def rows(h):
        return pl.ds(h * HALF, HALF)

    def piece(s, h):
        return wall.at[s, rows(h)]

    def send_own(h, peer):
        pltpu.make_async_remote_copy(
            src_ref=w_hbm.at[rows(h)], dst_ref=piece(me, h), send_sem=wsend, recv_sem=wrecv.at[me, h],
            device_id=peer, device_id_type=MESH,
        ).start()

    def send(s, h, peer):
        pltpu.make_async_remote_copy(
            src_ref=piece(s, h), dst_ref=piece(s, h), send_sem=wsend, recv_sem=wrecv.at[s, h],
            device_id=peer, device_id_type=MESH,
        ).start()

    def arrived(s, h):
        pltpu.make_async_remote_copy(
            src_ref=piece(s, h), dst_ref=piece(s, h), send_sem=wsend, recv_sem=wrecv.at[s, h],
            device_id=z_peer, device_id_type=MESH,
        ).wait_recv()

    pl.semaphore_wait(barrier, 7)
    send_own(0, z_peer)
    send_own(0, a_up)
    send_own(1, a_dn)
    send_own(0, b_up)
    send_own(1, b_dn)
    send_own(1, z_peer)
    send_own(1, a_up)
    send_own(0, a_dn)
    send_own(1, b_up)
    send_own(0, b_dn)
    og_copy.start()

    t_col = lax.broadcasted_iota(jnp.int32, (tok, HD), 0)
    begin = jnp.zeros((tok, HD), jnp.int32)
    at = jnp.int32(0)
    for d in range(len_ref.shape[1]):
        begin = jnp.where(t_col >= at, at, begin)
        at = at + len_ref[0, d]
    start_t[...] = begin
    angle = (t_col - begin).astype(F32) * freq_ref[0:1, :]
    cos_t[...] = jnp.cos(angle)
    sin_t[...] = jnp.sin(angle) * freq_ref[1:2, :]

    def rotated(field, lo, n):
        f = field.astype(F32)
        return (f * cos_t[pl.ds(lo, n), :] + pltpu.roll(f, HD // 2, 1) * sin_t[pl.ds(lo, n), :]).astype(BF16)

    k_copy.wait()
    kall[pl.ds(prompt, tok), :] = rotated(kin[...], 0, tok)
    for c in (pk_copy, q_copy, pv_copy, v_copy, w_copy):
        c.wait()
    acc[...] = jnp.zeros_like(acc)

    def attention(i):
        lo = max(0, i - (DOC_MOST + TILE - 2) // TILE) * TILE
        n = (i + 1) * TILE - lo
        r = pl.ds(i * TILE, TILE)
        nt = (((1,), (1,)), ((), ()))

        def head(h, carry):
            lanes = pl.ds(pl.multiple_of(h * HD, HD), HD)
            q = rotated(qin[r, lanes], i * TILE, TILE)
            qrot[r, lanes] = q
            s_p = lax.dot_general(q, kall[pl.ds(0, prompt), :], nt, preferred_element_type=F32)
            s_t = lax.dot_general(q, kall[pl.ds(prompt + lo, n), :], nt, preferred_element_type=F32)
            col = lax.broadcasted_iota(jnp.int32, (TILE, n), 1) + lo
            row = lax.broadcasted_iota(jnp.int32, (TILE, n), 0) + i * TILE
            seen = (col <= row) & (col >= start_t[r, 0:1])
            s_t = jnp.where(seen, s_t, -1e30)
            top = jnp.maximum(jnp.max(s_p, axis=1, keepdims=True), jnp.max(s_t, axis=1, keepdims=True))
            e_p = jnp.exp((s_p - top) * scale)
            e_t = jnp.exp((s_t - top) * scale)
            inv = 1.0 / (jnp.sum(e_p, axis=1, keepdims=True) + jnp.sum(e_t, axis=1, keepdims=True))
            o = jnp.dot(e_p.astype(BF16), vall[pl.ds(0, prompt), :], preferred_element_type=F32)
            o = o + jnp.dot(e_t.astype(BF16), vall[pl.ds(prompt + lo, n), :], preferred_element_type=F32)
            attn[r, lanes] = (o * inv).astype(BF16)
            prob_t[lanes, r] = jnp.transpose(e_p * inv).astype(BF16)
            return carry

        lax.fori_loop(0, heads, head, 0, unroll=2)

    def both(s):
        arrived(s, 0)
        arrived(s, 1)

    attention(0)
    attention(1)
    arrived(slot(0, -1, 0), 0)
    send(slot(0, -1, 0), 0, a_up)
    arrived(slot(0, 1, 0), 1)
    send(slot(0, 1, 0), 1, a_dn)
    other = slot(1, 0, 0)
    for h in range(2):
        arrived(other, h)
        send(other, h, b_up)
        send(other, h, b_dn)
        send(other, h, a_up)
        send(other, h, a_dn)
        attention(2 + h)
    arrived(slot(0, -1, 0), 1)
    arrived(slot(0, 1, 0), 0)
    for h in range(2):
        send(slot(0, 1, 0), h, b_up)
        send(slot(0, -1, 0), h, b_dn)
    attention(4)
    both(slot(1, 0, -1))
    both(slot(1, 0, 1))
    send(slot(1, 0, -1), 0, b_up)
    send(slot(1, 0, 1), 1, b_dn)
    for h in range(2):
        send(slot(1, 0, 1), h, a_up)
        send(slot(1, 0, -1), h, a_dn)
    og_copy.wait()

    def slot_of(step, table, j):
        kind = 0 if j < 2 else 1
        return slot(kind, pick(step, [t[j][1] for t in table]), pick(step, [t[j][2] for t in table]))

    def tick(t):
        up, dn = slot_of(t, TICKS, 0), slot_of(t, TICKS, 1)
        up2, dn2 = slot_of(t, TICKS, 2), slot_of(t, TICKS, 3)
        for h in range(2):
            send(up, h, b_up)
            send(dn, h, b_dn)
            send(up2, h, a_up)
            send(dn2, h, a_dn)

    def unit(step, j):
        i = step * 4 + jnp.where((step >= 4) & (zl == zh), (j + 2) % 4, j)
        flat = [u for four in STEPS for u in four]
        return slot(pick(i, [u[0] for u in flat]), pick(i, [u[1] for u in flat]), pick(i, [u[2] for u in flat]))

    def index_of(s):
        return (s // 16) * 8 + ((s // 4) % 2) * 4 + s % 4

    def core_copy(s):
        n = index_of(s)
        return pltpu.make_async_remote_copy(
            src_ref=part.at[s], dst_ref=rbuf.at[n], send_sem=csend, recv_sem=crecv.at[n],
            device_id=c_peer, device_id_type=MESH,
        )

    def far_copy(s):
        n = index_of(s) % 8
        return pltpu.make_async_remote_copy(
            src_ref=part.at[s], dst_ref=zbuf.at[n], send_sem=zsend, recv_sem=zrecv.at[n],
            device_id=far_peer, device_id_type=MESH,
        )

    def columns(n):
        return pl.ds(pl.multiple_of(n * UNIT, UNIT), UNIT)

    def hand_over(s):
        @pl.when((s // 8) % 2 != core)
        def _():
            core_copy(s).start()

    def add_grads(step, lo, hi):
        four = [unit(step, j) for j in range(4)]
        g = jnp.concatenate([og[:, columns(s)] for s in four], axis=1)
        for b in range(lo // UNIT, hi // UNIT):
            w = jnp.concatenate([wall[s, b * UNIT:(b + 1) * UNIT, :] for s in four], axis=1)
            acc[:, b * UNIT:(b + 1) * UNIT] += lax.dot_general(
                g, w, (((1,), (1,)), ((), ())), preferred_element_type=F32
            )

    def process(s):
        part[s] = jnp.dot(attn[...], wall[s], preferred_element_type=F32).astype(BF16)
        hand_over(s)

    def combine(s):
        @pl.when((s // 8) % 2 == core)
        def _():
            n = index_of(s)
            core_copy(s).wait_recv()
            part[s] = (part[s].astype(F32) + rbuf[n].astype(F32)).astype(BF16)

            @pl.when(s // 16 != zh)
            def _():
                far_copy(s).start()

    def finish(i, c):
        s = unit(i // 4, i % 4)

        @pl.when(((s // 8) % 2 == core) & (s // 16 == zh))
        def _():
            n = index_of(s) % 8
            far_copy(s).wait_recv()
            out_ref[:, columns(n)] = (part[s].astype(F32) + zbuf[n].astype(F32)).astype(BF16)

        return c

    def step_body(step, carry):
        @pl.when(step == 1)
        def _():
            both(slot(0, 0, 1))
            both(slot(0, 0, -1))
            both(slot(0, 2, 0))
            tick(1)

        @pl.when(step == 2)
        def _():
            both(slot(1, 1, 0))
            both(slot(1, -1, 0))
            both(slot(0, 1, -1))

        @pl.when((step >= 3) & (step <= 5))
        def _():
            for j in range(4):
                both(unit(step, j))
            tick(step - 1)

        def one(j, c):
            s = unit(step, j)

            @pl.when(step == 6)
            def _():
                both(s)

            process(s)

            @pl.when(j > 0)
            def _():
                combine(unit(step, j - 1))

            return c

        lax.fori_loop(0, 4, one, 0)
        add_grads(step, 0, acc.shape[1])
        combine(unit(step, 3))

        @pl.when(step >= 2)
        def _():
            lax.fori_loop(4 * (step - 2), 4 * (step - 1), finish, 0)

        return carry

    lax.fori_loop(0, 7, step_body, 0)

    nn = (((1,), (0,)), ((), ()))
    nt = (((1,), (1,)), ((), ()))
    kg[...] = jnp.zeros_like(kg)
    vg[...] = jnp.zeros_like(vg)

    def grads(h, c):
        lanes = pl.ds(pl.multiple_of(h * HD, HD), HD)
        g32 = acc[:, lanes].astype(BF16).astype(F32)
        g = g32.astype(BF16)
        p = prob_t[lanes, :]
        weighed = (g32 * attn[:, lanes].astype(F32)).astype(BF16)
        delta = lax.dot_general(jnp.ones((8, HD), BF16), weighed, nt, preferred_element_type=F32)[0:1, :]
        gp = lax.dot_general(vall[pl.ds(0, prompt), :], g, nt, preferred_element_type=F32)
        ds = (p.astype(F32) * (gp - delta) * scale).astype(BF16)
        kg[...] += lax.dot_general(ds, qrot[:, lanes], nn, preferred_element_type=F32)
        vg[...] += lax.dot_general(p, g, nn, preferred_element_type=F32)
        return c

    def first_half(j, c):
        s = unit(7, j)
        arrived(s, 0)
        part[s] = jnp.dot(attn[:, 0:HALF], wall[s, 0:HALF, :], preferred_element_type=F32).astype(BF16)
        return c

    lax.fori_loop(0, 4, first_half, 0)
    add_grads(7, 0, HALF)
    lax.fori_loop(0, heads // 2, grads, 0, unroll=4)

    lax.fori_loop(20, 24, finish, 0)

    def second_product(j, c):
        s = unit(7, j)
        rest = jnp.dot(attn[:, HALF:2 * HALF], wall[s, HALF:2 * HALF, :], preferred_element_type=F32)
        part[s] = (part[s].astype(F32) + rest).astype(BF16)
        hand_over(s)
        return c

    def leaving(j, c):
        arrived(unit(7, j), 1)
        return second_product(j, c)

    lax.fori_loop(0, 2, leaving, 0)

    arrived(unit(7, 2), 1)
    arrived(unit(7, 3), 1)
    add_grads(7, HALF, 2 * HALF)
    combine(unit(7, 0))
    combine(unit(7, 1))
    lax.fori_loop(heads // 2, heads, grads, 0, unroll=4)

    n_dp = gsend.shape[0]
    own_rows = prompt // n_dp
    gsend[:, 0:own_rows, :] = kg[...].reshape(n_dp, own_rows, HD)
    gsend[:, own_rows:2 * own_rows, :] = vg[...].reshape(n_dp, own_rows, HD)

    def grad_send(j, c):
        pltpu.make_async_remote_copy(
            src_ref=gsend.at[(dp + j) % n_dp], dst_ref=grecv.at[dp], send_sem=gssem, recv_sem=grsem,
            device_id=((dp + j) % n_dp, mp), device_id_type=MESH,
        ).start()
        return c

    lax.fori_loop(1, n_dp, grad_send, 0)
    grecv[dp] = gsend[dp]
    lax.fori_loop(2, 4, second_product, 0)

    lax.fori_loop(24, 28, finish, 0)
    combine(unit(7, 2))
    combine(unit(7, 3))

    everyone = pltpu.make_async_remote_copy(
        src_ref=gsend.at[pl.ds(0, n_dp - 1)], dst_ref=grecv.at[pl.ds(0, n_dp - 1)], send_sem=gssem, recv_sem=grsem,
        device_id=z_peer, device_id_type=MESH,
    )
    everyone.wait_recv()
    total = jnp.sum(grecv[...], axis=0)
    kg_out[...] = total[0:own_rows, :]
    vg_out[...] = total[own_rows:2 * own_rows, :]
    everyone.wait_send()
    lax.fori_loop(28, 32, finish, 0)
    for buf, sem in ((wall.at[pl.ds(0, n_dp - 1)], wsend), (rbuf, csend), (zbuf, zsend)):
        pltpu.make_async_remote_copy(
            src_ref=buf, dst_ref=buf, send_sem=sem, recv_sem=wrecv.at[0, 0], device_id=z_peer, device_id_type=MESH
        ).wait_send()


def write_out(*refs):
    n = len(refs) // 2
    copies = [pltpu.make_async_copy(refs[i], refs[n + i], refs[2 * n].at[i]) for i in range(n)]
    for c in copies:
        c.start()
    for c in copies:
        c.wait()


def per_device(queries, keys, values, prompt_keys, prompt_values, out_weight, out_grad, lengths):
    tok, width = queries.shape
    prompt = prompt_keys.shape[0]
    n_dp = lax.axis_size("dp")
    own_rows = prompt // n_dp
    half = HD // 2
    freq = ROPE_BASE ** (-2.0 * np.arange(half) / HD)
    table = np.zeros((8, HD), np.float32)
    table[0] = np.concatenate([freq, freq])
    table[1] = np.concatenate([-np.ones(half), np.ones(half)])
    anywhere = pl.BlockSpec(memory_space=pl.ANY)
    vmem = pl.BlockSpec(memory_space=pltpu.VMEM)
    dma = pltpu.SemaphoreType.DMA
    results = pl.pallas_call(
        kernel,
        out_shape=(
            pltpu.VMEM((tok, 8 * UNIT), BF16),
            pltpu.VMEM((own_rows, HD), F32),
            pltpu.VMEM((own_rows, HD), F32),
        ),
        in_specs=[anywhere] * 7 + [pl.BlockSpec(memory_space=pltpu.SMEM), vmem],
        out_specs=(vmem, vmem, vmem),
        scratch_shapes=[
            pltpu.VMEM((n_dp, width, UNIT), BF16),
            pltpu.VMEM((tok, n_dp * UNIT), BF16),
            pltpu.VMEM((n_dp, tok, UNIT), BF16),
            pltpu.VMEM((16, tok, UNIT), BF16),
            pltpu.VMEM((8, tok, UNIT), BF16),
            pltpu.VMEM((prompt, HD), F32),
            pltpu.VMEM((prompt, HD), F32),
            pltpu.VMEM((n_dp, 2 * own_rows, HD), F32),
            pltpu.VMEM((n_dp, 2 * own_rows, HD), F32),
            pltpu.VMEM((tok, width), F32),
            pltpu.VMEM((tok, width), BF16),
            pltpu.VMEM((tok, width), BF16),
            pltpu.VMEM((width, tok), BF16),
            pltpu.VMEM((tok, width), BF16),
            pltpu.VMEM((tok, HD), BF16),
            pltpu.VMEM((prompt + tok, HD), BF16),
            pltpu.VMEM((prompt + tok, HD), BF16),
            pltpu.VMEM((tok, HD), F32),
            pltpu.VMEM((tok, HD), F32),
            pltpu.VMEM((tok, HD), jnp.int32),
            dma((7,)),
            dma,
            dma((n_dp, 2)),
            dma,
            dma((16,)),
            dma,
            dma((8,)),
            dma,
            dma,
        ],
        compiler_params=pltpu.CompilerParams(
            collective_id=0, has_side_effects=True, vmem_limit_bytes=58 * 1024 * 1024
        ),
    )(queries, keys, values, prompt_keys, prompt_values, out_weight, out_grad, lengths, jnp.asarray(table))
    return pl.pallas_call(
        write_out,
        out_shape=tuple(jax.ShapeDtypeStruct(r.shape, r.dtype) for r in results),
        in_specs=[vmem] * 3,
        out_specs=(anywhere,) * 3,
        scratch_shapes=[dma((3,))],
    )(*(pltpu.with_memory_space_constraint(r, pltpu.VMEM) for r in results))


def solution(mesh):
    in_specs = (
        P("dp", "mp"),
        P("dp", "mp"),
        P("dp", "mp"),
        P(None, "mp"),
        P(None, "mp"),
        P("mp", "dp"),
        P("dp", None),
        P("dp", None),
    )
    out_specs = (P("dp", "mp"), P("dp", "mp"), P("dp", "mp"))
    return jax.shard_map(
        per_device, mesh=mesh, in_specs=in_specs, out_specs=out_specs, check_vma=False
    )
```

```python
import functools
import math

import jax
import jax.numpy as jnp
import numpy as np
from jax import lax
from jax.experimental import pallas as pl
from jax.experimental.pallas import tpu as pltpu
from jax.sharding import PartitionSpec as P

HD = 128
DOC_MOST = 320
ROPE_BASE = 1000000.0
TILE = 128
HALF = 512
UNIT = 256
MESH = pl.DeviceIdType.MESH
F32 = jnp.float32
BF16 = jnp.bfloat16


def pick(i, values):
    out = values[0]
    for k in range(1, len(values)):
        out = jnp.where(i == k, values[k], out)
    return out


STEPS = [
    [(0, 0, 0), (0, 1, 0), (0, -1, 0), (1, 0, 0)],
    [(0, 0, 1), (0, 0, -1), (0, 2, 0), (1, 0, 1)],
    [(1, 0, -1), (1, 1, 0), (1, -1, 0), (0, 1, -1)],
    [(0, -1, 1), (1, 0, 2), (1, -1, 1), (1, 1, -1)],
    [(0, -1, -1), (0, 2, 1), (1, -1, -1), (1, 1, 1)],
    [(0, 2, -1), (0, 1, 1), (1, -1, 2), (1, 1, 2)],
    [(0, 0, 2), (0, -1, 2), (1, 2, 0), (1, 2, -1)],
    [(0, 1, 2), (0, 2, 2), (1, 2, 1), (1, 2, 2)],
]
TICKS = [
    [(0, 1, 0), (0, -1, 0), (1, 0, 1), (1, 0, -1)],
    [(0, -1, 0), (0, 2, 0), (1, 0, -1), (1, 0, 1)],
    [(0, 2, 0), (0, 1, 0), (1, 0, 2), (1, 0, 2)],
    [(0, 0, -1), (0, -1, 1), (1, -1, 0), (1, 1, -1)],
    [(0, 1, -1), (0, 2, 1), (1, -1, 1), (1, 1, 2)],
]


def kernel(
    q_hbm, k_hbm, v_hbm, pk_hbm, pv_hbm, w_hbm, og_hbm, len_ref, freq_ref,
    out_ref, kg_out, vg_out,
    wall, og, part, rbuf, zbuf, kg, vg, gsend, grecv, acc, attn, qrot, prob_t, qin, kin, kall, vall, cos_t, sin_t, start_t,
    in_sem, wsend, wrecv, csend, crecv, zsend, zrecv, gssem, grsem,
):
    tok = q_hbm.shape[0]
    heads = q_hbm.shape[1] // HD
    prompt = pk_hbm.shape[0]
    n_tiles = tok // TILE
    scale = HD ** -0.5
    dp = lax.axis_index("dp")
    mp = lax.axis_index("mp")
    x0, y0, zl = dp % 4, (dp // 4) % 4, dp // 16
    zh, core = mp // 2, mp % 2

    def dpid(x, y, z):
        return z * 16 + y * 4 + x

    def pa(d):
        x = jnp.where(zl == 0, (x0 + d) % 4, x0)
        y = jnp.where(zl == 0, y0, (y0 + d) % 4)
        return (dpid(x, y, zl), mp)

    def pb(d):
        x = jnp.where(zl == 0, x0, (x0 + d) % 4)
        y = jnp.where(zl == 0, (y0 + d) % 4, y0)
        return (dpid(x, y, zl), mp)

    def slot(kind, da, db):
        x = (x0 + jnp.where(zl == 0, da, db) + 4) % 4
        y = (y0 + jnp.where(zl == 0, db, da) + 4) % 4
        t = jnp.where(kind == 0, zl, 1 - zl)
        return t * 16 + y * 4 + x

    a_up, a_dn, b_up, b_dn = pa(1), pa(3), pb(1), pb(3)
    z_peer = (dpid(x0, y0, 1 - zl), mp)
    c_peer = (dp, zh * 2 + 1 - core)
    far_peer = (dp, (1 - zh) * 2 + core)

    barrier = pltpu.get_barrier_semaphore()
    for peer in (a_up, a_dn, b_up, b_dn, z_peer, c_peer, far_peer):
        pl.semaphore_signal(barrier, inc=1, device_id=peer, device_id_type=MESH)

    me = slot(0, 0, 0)
    q_copy = pltpu.make_async_copy(q_hbm, qin, in_sem.at[0])
    k_copy = pltpu.make_async_copy(k_hbm, kin, in_sem.at[1])
    pk_copy = pltpu.make_async_copy(pk_hbm, kall.at[pl.ds(0, prompt)], in_sem.at[2])
    pv_copy = pltpu.make_async_copy(pv_hbm, vall.at[pl.ds(0, prompt)], in_sem.at[3])
    v_copy = pltpu.make_async_copy(v_hbm, vall.at[pl.ds(prompt, tok)], in_sem.at[4])
    w_copy = pltpu.make_async_copy(w_hbm, wall.at[me], in_sem.at[5])
    og_copy = pltpu.make_async_copy(og_hbm, og, in_sem.at[6])
    w_copy.start()
    for c in (k_copy, pk_copy, q_copy, pv_copy, v_copy):
        c.start()

    def rows(h):
        return pl.ds(h * HALF, HALF)

    def piece(s, h):
        return wall.at[s, rows(h)]

    def send_own(h, peer):
        pltpu.make_async_remote_copy(
            src_ref=w_hbm.at[rows(h)], dst_ref=piece(me, h), send_sem=wsend, recv_sem=wrecv.at[me, h],
            device_id=peer, device_id_type=MESH,
        ).start()

    def send(s, h, peer):
        pltpu.make_async_remote_copy(
            src_ref=piece(s, h), dst_ref=piece(s, h), send_sem=wsend, recv_sem=wrecv.at[s, h],
            device_id=peer, device_id_type=MESH,
        ).start()

    def arrived(s, h):
        pltpu.make_async_remote_copy(
            src_ref=piece(s, h), dst_ref=piece(s, h), send_sem=wsend, recv_sem=wrecv.at[s, h],
            device_id=z_peer, device_id_type=MESH,
        ).wait_recv()

    def quarter_copy(s, r, c, peer):
        quarter = wall.at[s, rows(r), pl.ds(c * HD, HD)]
        return pltpu.make_async_remote_copy(
            src_ref=quarter, dst_ref=quarter, send_sem=wsend, recv_sem=wrecv.at[s, 2 * c + r],
            device_id=peer, device_id_type=MESH,
        )

    pl.semaphore_wait(barrier, 7)
    send_own(0, z_peer)
    send_own(0, a_up)
    send_own(1, a_dn)
    send_own(0, b_up)
    send_own(1, b_dn)
    send_own(1, z_peer)
    send_own(1, a_up)
    send_own(0, a_dn)
    send_own(1, b_up)
    send_own(0, b_dn)
    og_copy.start()

    t_col = lax.broadcasted_iota(jnp.int32, (tok, HD), 0)
    begin = jnp.zeros((tok, HD), jnp.int32)
    at = jnp.int32(0)
    for d in range(len_ref.shape[1]):
        begin = jnp.where(t_col >= at, at, begin)
        at = at + len_ref[0, d]
    start_t[...] = begin
    angle = (t_col - begin).astype(F32) * freq_ref[0:1, :]
    cos_t[...] = jnp.cos(angle)
    sin_t[...] = jnp.sin(angle) * freq_ref[1:2, :]

    def rotated(field, lo, n):
        f = field.astype(F32)
        return (f * cos_t[pl.ds(lo, n), :] + pltpu.roll(f, HD // 2, 1) * sin_t[pl.ds(lo, n), :]).astype(BF16)

    k_copy.wait()
    kall[pl.ds(prompt, tok), :] = rotated(kin[...], 0, tok)
    for c in (pk_copy, q_copy, pv_copy, v_copy, w_copy):
        c.wait()
    acc[...] = jnp.zeros_like(acc)

    def attention(i):
        lo = max(0, i - (DOC_MOST + TILE - 2) // TILE) * TILE
        n = (i + 1) * TILE - lo
        r = pl.ds(i * TILE, TILE)
        nt = (((1,), (1,)), ((), ()))

        def head(h, carry):
            lanes = pl.ds(pl.multiple_of(h * HD, HD), HD)
            q = rotated(qin[r, lanes], i * TILE, TILE)
            qrot[r, lanes] = q
            s_p = lax.dot_general(q, kall[pl.ds(0, prompt), :], nt, preferred_element_type=F32)
            s_t = lax.dot_general(q, kall[pl.ds(prompt + lo, n), :], nt, preferred_element_type=F32)
            col = lax.broadcasted_iota(jnp.int32, (TILE, n), 1) + lo
            row = lax.broadcasted_iota(jnp.int32, (TILE, n), 0) + i * TILE
            seen = (col <= row) & (col >= start_t[r, 0:1])
            s_t = jnp.where(seen, s_t, -1e30)
            top = jnp.maximum(jnp.max(s_p, axis=1, keepdims=True), jnp.max(s_t, axis=1, keepdims=True))
            e_p = jnp.exp((s_p - top) * scale)
            e_t = jnp.exp((s_t - top) * scale)
            inv = 1.0 / (jnp.sum(e_p, axis=1, keepdims=True) + jnp.sum(e_t, axis=1, keepdims=True))
            o = jnp.dot(e_p.astype(BF16), vall[pl.ds(0, prompt), :], preferred_element_type=F32)
            o = o + jnp.dot(e_t.astype(BF16), vall[pl.ds(prompt + lo, n), :], preferred_element_type=F32)
            attn[r, lanes] = (o * inv).astype(BF16)
            prob_t[lanes, r] = jnp.transpose(e_p * inv).astype(BF16)
            return carry

        lax.fori_loop(0, heads, head, 0, unroll=2)

    def both(s):
        arrived(s, 0)
        arrived(s, 1)

    attention(0)
    attention(1)
    arrived(slot(0, -1, 0), 0)
    send(slot(0, -1, 0), 0, a_up)
    arrived(slot(0, 1, 0), 1)
    send(slot(0, 1, 0), 1, a_dn)
    other = slot(1, 0, 0)
    for h in range(2):
        arrived(other, h)
        send(other, h, b_up)
        send(other, h, b_dn)
        send(other, h, a_up)
        send(other, h, a_dn)
        attention(2 + h)
    arrived(slot(0, -1, 0), 1)
    arrived(slot(0, 1, 0), 0)
    for h in range(2):
        send(slot(0, 1, 0), h, b_up)
        send(slot(0, -1, 0), h, b_dn)
    attention(4)
    both(slot(1, 0, -1))
    both(slot(1, 0, 1))
    send(slot(1, 0, -1), 0, b_up)
    send(slot(1, 0, 1), 1, b_dn)
    for h in range(2):
        send(slot(1, 0, 1), h, a_up)
        send(slot(1, 0, -1), h, a_dn)
    og_copy.wait()

    def slot_of(step, table, j):
        kind = 0 if j < 2 else 1
        return slot(kind, pick(step, [t[j][1] for t in table]), pick(step, [t[j][2] for t in table]))

    def tick(t):
        up, dn = slot_of(t, TICKS, 0), slot_of(t, TICKS, 1)
        up2, dn2 = slot_of(t, TICKS, 2), slot_of(t, TICKS, 3)
        for h in range(2):
            send(up, h, b_up)
            send(dn, h, b_dn)
            send(up2, h, a_up)
            send(dn2, h, a_dn)

    def last_tick():
        on_b = ((slot_of(4, TICKS, 0), b_up), (slot_of(4, TICKS, 1), b_dn))
        on_a = ((slot_of(4, TICKS, 2), a_up), (slot_of(4, TICKS, 3), a_dn))

        def go(leave, stay):
            for c in range(2):
                for r in range(2):
                    for s, peer in leave:
                        quarter_copy(s, r, c, peer).start()
                for s, peer in stay:
                    send(s, c, peer)

        @pl.when(zl == zh)
        def _():
            go(on_a, on_b)

        @pl.when(zl != zh)
        def _():
            go(on_b, on_a)

    def unit(step, j):
        i = step * 4 + jnp.where((step >= 4) & (zl == zh), (j + 2) % 4, j)
        flat = [u for four in STEPS for u in four]
        return slot(pick(i, [u[0] for u in flat]), pick(i, [u[1] for u in flat]), pick(i, [u[2] for u in flat]))

    def index_of(s):
        return (s // 16) * 8 + ((s // 4) % 2) * 4 + s % 4

    def part_of(c):
        return pl.ds(0, UNIT) if c is None else pl.ds(c * HD, HD)

    def core_copy(s, c=None):
        n = index_of(s)
        return pltpu.make_async_remote_copy(
            src_ref=part.at[s, :, part_of(c)], dst_ref=rbuf.at[n, :, part_of(c)], send_sem=csend,
            recv_sem=crecv.at[n, c or 0], device_id=c_peer, device_id_type=MESH,
        )

    def far_copy(s, c=None):
        n = index_of(s) % 8
        return pltpu.make_async_remote_copy(
            src_ref=part.at[s, :, part_of(c)], dst_ref=zbuf.at[n, :, part_of(c)], send_sem=zsend,
            recv_sem=zrecv.at[n, c or 0], device_id=far_peer, device_id_type=MESH,
        )

    def columns(n):
        return pl.ds(pl.multiple_of(n * UNIT, UNIT), UNIT)

    def hand_over(s, c=None):
        @pl.when((s // 8) % 2 != core)
        def _():
            core_copy(s, c).start()

    def add_grads(step, lo, hi):
        four = [unit(step, j) for j in range(4)]
        g = jnp.concatenate([og[:, columns(s)] for s in four], axis=1)
        for b in range(lo // UNIT, hi // UNIT):
            w = jnp.concatenate([wall[s, b * UNIT:(b + 1) * UNIT, :] for s in four], axis=1)
            acc[:, b * UNIT:(b + 1) * UNIT] += lax.dot_general(
                g, w, (((1,), (1,)), ((), ())), preferred_element_type=F32
            )

    def process(s):
        part[s] = jnp.dot(attn[...], wall[s], preferred_element_type=F32).astype(BF16)
        hand_over(s)

    def combine(s, c=None):
        @pl.when((s // 8) % 2 == core)
        def _():
            n = index_of(s)
            core_copy(s, c).wait_recv()
            p = part_of(c)
            part[s, :, p] = (part[s, :, p].astype(F32) + rbuf[n, :, p].astype(F32)).astype(BF16)

            @pl.when(s // 16 != zh)
            def _():
                far_copy(s, c).start()

    def finish_of(s, c=None):
        @pl.when(((s // 8) % 2 == core) & (s // 16 == zh))
        def _():
            n = index_of(s) % 8
            far_copy(s, c).wait_recv()
            p = part_of(c)
            at = 0 if c is None else c * HD
            wide = UNIT if c is None else HD
            out_ref[:, pl.ds(pl.multiple_of(n * UNIT + at, HD), wide)] = (
                part[s, :, p].astype(F32) + zbuf[n, :, p].astype(F32)
            ).astype(BF16)

    def finish(i, carry):
        finish_of(unit(i // 4, i % 4))
        return carry

    def step_body(step, carry):
        @pl.when(step == 1)
        def _():
            both(slot(0, 0, 1))
            both(slot(0, 0, -1))
            both(slot(0, 2, 0))
            tick(1)

        @pl.when(step == 2)
        def _():
            both(slot(1, 1, 0))
            both(slot(1, -1, 0))
            both(slot(0, 1, -1))

        @pl.when((step >= 3) & (step <= 5))
        def _():
            for j in range(4):
                both(unit(step, j))

        @pl.when((step >= 3) & (step <= 4))
        def _():
            tick(step - 1)

        @pl.when(step == 5)
        def _():
            last_tick()

        def one(j, c):
            s = unit(step, j)

            @pl.when(step == 6)
            def _():
                both(s)

            process(s)

            @pl.when(j > 0)
            def _():
                combine(unit(step, j - 1))

            return c

        lax.fori_loop(0, 4, one, 0)
        add_grads(step, 0, acc.shape[1])
        combine(unit(step, 3))

        @pl.when(step >= 2)
        def _():
            lax.fori_loop(4 * (step - 2), 4 * (step - 1), finish, 0)

        return carry

    lax.fori_loop(0, 7, step_body, 0)

    nn = (((1,), (0,)), ((), ()))
    nt = (((1,), (1,)), ((), ()))
    kg[...] = jnp.zeros_like(kg)
    vg[...] = jnp.zeros_like(vg)

    def grads(h, c):
        lanes = pl.ds(pl.multiple_of(h * HD, HD), HD)
        g32 = acc[:, lanes].astype(BF16).astype(F32)
        g = g32.astype(BF16)
        p = prob_t[lanes, :]
        weighed = (g32 * attn[:, lanes].astype(F32)).astype(BF16)
        delta = lax.dot_general(jnp.ones((8, HD), BF16), weighed, nt, preferred_element_type=F32)[0:1, :]
        gp = lax.dot_general(vall[pl.ds(0, prompt), :], g, nt, preferred_element_type=F32)
        ds = (p.astype(F32) * (gp - delta) * scale).astype(BF16)
        kg[...] += lax.dot_general(ds, qrot[:, lanes], nn, preferred_element_type=F32)
        vg[...] += lax.dot_general(p, g, nn, preferred_element_type=F32)
        return c

    def last_arrived(j, r, c):
        quarter_copy(unit(7, j), r, c, z_peer).wait_recv()

    def leaving(c):
        def one(j, carry):
            s = unit(7, j)
            if c == 0:
                last_arrived(j, 0, 0)
            last_arrived(j, 1, c)
            part[s, :, part_of(c)] = jnp.dot(
                attn[...], wall[s, :, c * HD:(c + 1) * HD], preferred_element_type=F32
            ).astype(BF16)
            hand_over(s, c)
            return carry

        lax.fori_loop(0, 2, one, 0)

    def first_half(j, c):
        s = unit(7, j)
        arrived(s, 0)
        part[s] = jnp.dot(attn[:, 0:HALF], wall[s, 0:HALF, :], preferred_element_type=F32).astype(BF16)
        return c

    def second_product(j, c):
        s = unit(7, j)
        rest = jnp.dot(attn[:, HALF:2 * HALF], wall[s, HALF:2 * HALF, :], preferred_element_type=F32)
        part[s] = (part[s].astype(F32) + rest).astype(BF16)
        hand_over(s)
        return c

    leaving(0)
    lax.fori_loop(2, 4, first_half, 0)
    combine(unit(7, 0), 0)
    combine(unit(7, 1), 0)
    lax.fori_loop(20, 24, finish, 0)
    last_arrived(0, 0, 1)
    last_arrived(1, 0, 1)
    add_grads(7, 0, HALF)
    lax.fori_loop(0, heads // 2, grads, 0, unroll=4)
    leaving(1)
    arrived(unit(7, 2), 1)
    arrived(unit(7, 3), 1)
    add_grads(7, HALF, 2 * HALF)
    combine(unit(7, 0), 1)
    combine(unit(7, 1), 1)
    lax.fori_loop(heads // 2, heads, grads, 0, unroll=4)

    n_dp = gsend.shape[0]
    own_rows = prompt // n_dp
    gsend[:, 0:own_rows, :] = kg[...].reshape(n_dp, own_rows, HD)
    gsend[:, own_rows:2 * own_rows, :] = vg[...].reshape(n_dp, own_rows, HD)

    def grad_send(j, c):
        pltpu.make_async_remote_copy(
            src_ref=gsend.at[(dp + j) % n_dp], dst_ref=grecv.at[dp], send_sem=gssem, recv_sem=grsem,
            device_id=((dp + j) % n_dp, mp), device_id_type=MESH,
        ).start()
        return c

    lax.fori_loop(1, n_dp, grad_send, 0)
    grecv[dp] = gsend[dp]
    lax.fori_loop(2, 4, second_product, 0)

    lax.fori_loop(24, 28, finish, 0)
    combine(unit(7, 2))
    combine(unit(7, 3))

    everyone = pltpu.make_async_remote_copy(
        src_ref=gsend.at[pl.ds(0, n_dp - 1)], dst_ref=grecv.at[pl.ds(0, n_dp - 1)], send_sem=gssem, recv_sem=grsem,
        device_id=z_peer, device_id_type=MESH,
    )
    everyone.wait_recv()
    total = jnp.sum(grecv[...], axis=0)
    kg_out[...] = total[0:own_rows, :]
    vg_out[...] = total[own_rows:2 * own_rows, :]
    everyone.wait_send()

    def last_finish(j, carry):
        finish_of(unit(7, j), 0)
        finish_of(unit(7, j), 1)
        return carry

    lax.fori_loop(2, 4, last_finish, 0)
    for buf, sem in ((wall.at[pl.ds(0, n_dp - 1)], wsend), (rbuf, csend), (zbuf, zsend)):
        pltpu.make_async_remote_copy(
            src_ref=buf, dst_ref=buf, send_sem=sem, recv_sem=wrecv.at[0, 0], device_id=z_peer, device_id_type=MESH
        ).wait_send()


def write_out(*refs):
    n = len(refs) // 2
    copies = [pltpu.make_async_copy(refs[i], refs[n + i], refs[2 * n].at[i]) for i in range(n)]
    for c in copies:
        c.start()
    for c in copies:
        c.wait()


def per_device(queries, keys, values, prompt_keys, prompt_values, out_weight, out_grad, lengths):
    tok, width = queries.shape
    prompt = prompt_keys.shape[0]
    n_dp = lax.axis_size("dp")
    own_rows = prompt // n_dp
    half = HD // 2
    freq = ROPE_BASE ** (-2.0 * np.arange(half) / HD)
    table = np.zeros((8, HD), np.float32)
    table[0] = np.concatenate([freq, freq])
    table[1] = np.concatenate([-np.ones(half), np.ones(half)])
    anywhere = pl.BlockSpec(memory_space=pl.ANY)
    vmem = pl.BlockSpec(memory_space=pltpu.VMEM)
    dma = pltpu.SemaphoreType.DMA
    results = pl.pallas_call(
        kernel,
        out_shape=(
            pltpu.VMEM((tok, 8 * UNIT), BF16),
            pltpu.VMEM((own_rows, HD), F32),
            pltpu.VMEM((own_rows, HD), F32),
        ),
        in_specs=[anywhere] * 7 + [pl.BlockSpec(memory_space=pltpu.SMEM), vmem],
        out_specs=(vmem, vmem, vmem),
        scratch_shapes=[
            pltpu.VMEM((n_dp, width, UNIT), BF16),
            pltpu.VMEM((tok, n_dp * UNIT), BF16),
            pltpu.VMEM((n_dp, tok, UNIT), BF16),
            pltpu.VMEM((16, tok, UNIT), BF16),
            pltpu.VMEM((8, tok, UNIT), BF16),
            pltpu.VMEM((prompt, HD), F32),
            pltpu.VMEM((prompt, HD), F32),
            pltpu.VMEM((n_dp, 2 * own_rows, HD), F32),
            pltpu.VMEM((n_dp, 2 * own_rows, HD), F32),
            pltpu.VMEM((tok, width), F32),
            pltpu.VMEM((tok, width), BF16),
            pltpu.VMEM((tok, width), BF16),
            pltpu.VMEM((width, tok), BF16),
            pltpu.VMEM((tok, width), BF16),
            pltpu.VMEM((tok, HD), BF16),
            pltpu.VMEM((prompt + tok, HD), BF16),
            pltpu.VMEM((prompt + tok, HD), BF16),
            pltpu.VMEM((tok, HD), F32),
            pltpu.VMEM((tok, HD), F32),
            pltpu.VMEM((tok, HD), jnp.int32),
            dma((7,)),
            dma,
            dma((n_dp, 4)),
            dma,
            dma((16, 2)),
            dma,
            dma((8, 2)),
            dma,
            dma,
        ],
        compiler_params=pltpu.CompilerParams(
            collective_id=0, has_side_effects=True, vmem_limit_bytes=58 * 1024 * 1024
        ),
    )(queries, keys, values, prompt_keys, prompt_values, out_weight, out_grad, lengths, jnp.asarray(table))
    return pl.pallas_call(
        write_out,
        out_shape=tuple(jax.ShapeDtypeStruct(r.shape, r.dtype) for r in results),
        in_specs=[vmem] * 3,
        out_specs=(anywhere,) * 3,
        scratch_shapes=[dma((3,))],
    )(*(pltpu.with_memory_space_constraint(r, pltpu.VMEM) for r in results))


def solution(mesh):
    in_specs = (
        P("dp", "mp"),
        P("dp", "mp"),
        P("dp", "mp"),
        P(None, "mp"),
        P(None, "mp"),
        P("mp", "dp"),
        P("dp", None),
        P("dp", None),
    )
    out_specs = (P("dp", "mp"), P("dp", "mp"), P("dp", "mp"))
    return jax.shard_map(
        per_device, mesh=mesh, in_specs=in_specs, out_specs=out_specs, check_vma=False
    )
```

```python
import functools
import math

import jax
import jax.numpy as jnp
import numpy as np
from jax import lax
from jax.experimental import pallas as pl
from jax.experimental.pallas import tpu as pltpu
from jax.sharding import PartitionSpec as P

HD = 128
DOC_MOST = 320
ROPE_BASE = 1000000.0
TILE = 128
HALF = 512
UNIT = 256
MESH = pl.DeviceIdType.MESH
F32 = jnp.float32
BF16 = jnp.bfloat16


def pick(i, values):
    out = values[0]
    for k in range(1, len(values)):
        out = jnp.where(i == k, values[k], out)
    return out


STEPS = [
    [(0, 0, 0), (0, 1, 0), (0, -1, 0), (1, 0, 0)],
    [(0, 0, 1), (0, 0, -1), (0, 2, 0), (1, 0, 1)],
    [(1, 0, -1), (1, 1, 0), (1, -1, 0), (0, 1, -1)],
    [(0, -1, 1), (1, 0, 2), (1, -1, 1), (1, 1, -1)],
    [(0, -1, -1), (0, 2, 1), (1, -1, -1), (1, 1, 1)],
    [(0, 2, -1), (0, 1, 1), (1, -1, 2), (1, 1, 2)],
    [(0, 0, 2), (0, -1, 2), (1, 2, 0), (1, 2, -1)],
    [(0, 1, 2), (0, 2, 2), (1, 2, 1), (1, 2, 2)],
]
TICKS = [
    [(0, 1, 0), (0, -1, 0), (1, 0, 1), (1, 0, -1)],
    [(0, -1, 0), (0, 2, 0), (1, 0, -1), (1, 0, 1)],
    [(0, 2, 0), (0, 1, 0), (1, 0, 2), (1, 0, 2)],
    [(0, 0, -1), (0, -1, 1), (1, -1, 0), (1, 1, -1)],
    [(0, 1, -1), (0, 2, 1), (1, -1, 1), (1, 1, 2)],
]


def kernel(
    q_hbm, k_hbm, v_hbm, pk_hbm, pv_hbm, w_hbm, og_hbm, len_ref, freq_ref,
    out_ref, kg_out, vg_out,
    wall, og, part, rbuf, zbuf, kg, vg, gsend, grecv, acc, attn, qrot, prob_t, qin, kin, kall, vall, cos_t, sin_t, start_t,
    in_sem, wsend, wrecv, csend, crecv, zsend, zrecv, gssem, grsem,
):
    tok = q_hbm.shape[0]
    heads = q_hbm.shape[1] // HD
    prompt = pk_hbm.shape[0]
    n_tiles = tok // TILE
    scale = HD ** -0.5
    dp = lax.axis_index("dp")
    mp = lax.axis_index("mp")
    x0, y0, zl = dp % 4, (dp // 4) % 4, dp // 16
    zh, core = mp // 2, mp % 2

    def dpid(x, y, z):
        return z * 16 + y * 4 + x

    def pa(d):
        x = jnp.where(zl == 0, (x0 + d) % 4, x0)
        y = jnp.where(zl == 0, y0, (y0 + d) % 4)
        return (dpid(x, y, zl), mp)

    def pb(d):
        x = jnp.where(zl == 0, x0, (x0 + d) % 4)
        y = jnp.where(zl == 0, (y0 + d) % 4, y0)
        return (dpid(x, y, zl), mp)

    def slot(kind, da, db):
        x = (x0 + jnp.where(zl == 0, da, db) + 4) % 4
        y = (y0 + jnp.where(zl == 0, db, da) + 4) % 4
        t = jnp.where(kind == 0, zl, 1 - zl)
        return t * 16 + y * 4 + x

    a_up, a_dn, b_up, b_dn = pa(1), pa(3), pb(1), pb(3)
    z_peer = (dpid(x0, y0, 1 - zl), mp)
    c_peer = (dp, zh * 2 + 1 - core)
    far_peer = (dp, (1 - zh) * 2 + core)

    barrier = pltpu.get_barrier_semaphore()
    for peer in (a_up, a_dn, b_up, b_dn, z_peer, c_peer, far_peer):
        pl.semaphore_signal(barrier, inc=1, device_id=peer, device_id_type=MESH)

    me = slot(0, 0, 0)
    q_copy = pltpu.make_async_copy(q_hbm, qin, in_sem.at[0])
    k_copy = pltpu.make_async_copy(k_hbm, kin, in_sem.at[1])
    pk_copy = pltpu.make_async_copy(pk_hbm, kall.at[pl.ds(0, prompt)], in_sem.at[2])
    pv_copy = pltpu.make_async_copy(pv_hbm, vall.at[pl.ds(0, prompt)], in_sem.at[3])
    v_copy = pltpu.make_async_copy(v_hbm, vall.at[pl.ds(prompt, tok)], in_sem.at[4])
    w_copy = pltpu.make_async_copy(w_hbm, wall.at[me], in_sem.at[5])
    og_copy = pltpu.make_async_copy(og_hbm, og, in_sem.at[6])
    w_copy.start()
    for c in (k_copy, pk_copy, q_copy, pv_copy, v_copy):
        c.start()

    def rows(h):
        return pl.ds(h * HALF, HALF)

    def piece(s, h):
        return wall.at[s, rows(h)]

    def send_own(h, peer):
        pltpu.make_async_remote_copy(
            src_ref=w_hbm.at[rows(h)], dst_ref=piece(me, h), send_sem=wsend, recv_sem=wrecv.at[me, h],
            device_id=peer, device_id_type=MESH,
        ).start()

    def send(s, h, peer):
        pltpu.make_async_remote_copy(
            src_ref=piece(s, h), dst_ref=piece(s, h), send_sem=wsend, recv_sem=wrecv.at[s, h],
            device_id=peer, device_id_type=MESH,
        ).start()

    def arrived(s, h):
        pltpu.make_async_remote_copy(
            src_ref=piece(s, h), dst_ref=piece(s, h), send_sem=wsend, recv_sem=wrecv.at[s, h],
            device_id=z_peer, device_id_type=MESH,
        ).wait_recv()

    def quarter_copy(s, r, c, peer):
        quarter = wall.at[s, rows(r), pl.ds(c * HD, HD)]
        return pltpu.make_async_remote_copy(
            src_ref=quarter, dst_ref=quarter, send_sem=wsend, recv_sem=wrecv.at[s, 2 * c + r],
            device_id=peer, device_id_type=MESH,
        )

    pl.semaphore_wait(barrier, 7)
    send_own(0, z_peer)
    send_own(0, a_up)
    send_own(1, a_dn)
    send_own(0, b_up)
    send_own(1, b_dn)
    send_own(1, z_peer)
    send_own(1, a_up)
    send_own(0, a_dn)
    send_own(1, b_up)
    send_own(0, b_dn)
    og_copy.start()

    t_col = lax.broadcasted_iota(jnp.int32, (tok, HD), 0)
    begin = jnp.zeros((tok, HD), jnp.int32)
    at = jnp.int32(0)
    for d in range(len_ref.shape[1]):
        begin = jnp.where(t_col >= at, at, begin)
        at = at + len_ref[0, d]
    start_t[...] = begin
    angle = (t_col - begin).astype(F32) * freq_ref[0:1, :]
    cos_t[...] = jnp.cos(angle)
    sin_t[...] = jnp.sin(angle) * freq_ref[1:2, :]

    def rotated(field, lo, n):
        f = field.astype(F32)
        return (f * cos_t[pl.ds(lo, n), :] + pltpu.roll(f, HD // 2, 1) * sin_t[pl.ds(lo, n), :]).astype(BF16)

    k_copy.wait()
    kall[pl.ds(prompt, tok), :] = rotated(kin[...], 0, tok)
    for c in (pk_copy, q_copy, pv_copy, v_copy, w_copy):
        c.wait()
    acc[...] = jnp.zeros_like(acc)

    def attention(i):
        lo = max(0, i - (DOC_MOST + TILE - 2) // TILE) * TILE
        n = (i + 1) * TILE - lo
        r = pl.ds(i * TILE, TILE)
        nt = (((1,), (1,)), ((), ()))

        def head(h, carry):
            lanes = pl.ds(pl.multiple_of(h * HD, HD), HD)
            q = rotated(qin[r, lanes], i * TILE, TILE)
            qrot[r, lanes] = q
            s_p = lax.dot_general(q, kall[pl.ds(0, prompt), :], nt, preferred_element_type=F32)
            s_t = lax.dot_general(q, kall[pl.ds(prompt + lo, n), :], nt, preferred_element_type=F32)
            col = lax.broadcasted_iota(jnp.int32, (TILE, n), 1) + lo
            row = lax.broadcasted_iota(jnp.int32, (TILE, n), 0) + i * TILE
            seen = (col <= row) & (col >= start_t[r, 0:1])
            s_t = jnp.where(seen, s_t, -1e30)
            top = jnp.maximum(jnp.max(s_p, axis=1, keepdims=True), jnp.max(s_t, axis=1, keepdims=True))
            e_p = jnp.exp((s_p - top) * scale)
            e_t = jnp.exp((s_t - top) * scale)
            inv = 1.0 / (jnp.sum(e_p, axis=1, keepdims=True) + jnp.sum(e_t, axis=1, keepdims=True))
            o = jnp.dot(e_p.astype(BF16), vall[pl.ds(0, prompt), :], preferred_element_type=F32)
            o = o + jnp.dot(e_t.astype(BF16), vall[pl.ds(prompt + lo, n), :], preferred_element_type=F32)
            attn[r, lanes] = (o * inv).astype(BF16)
            prob_t[lanes, r] = jnp.transpose(e_p * inv).astype(BF16)
            return carry

        lax.fori_loop(0, heads, head, 0, unroll=2)

    def both(s):
        arrived(s, 0)
        arrived(s, 1)

    attention(0)
    attention(1)
    arrived(slot(0, -1, 0), 0)
    send(slot(0, -1, 0), 0, a_up)
    arrived(slot(0, 1, 0), 1)
    send(slot(0, 1, 0), 1, a_dn)
    other = slot(1, 0, 0)
    for h in range(2):
        arrived(other, h)
        send(other, h, b_up)
        send(other, h, b_dn)
        send(other, h, a_up)
        send(other, h, a_dn)
        attention(2 + h)
    arrived(slot(0, -1, 0), 1)
    arrived(slot(0, 1, 0), 0)
    for h in range(2):
        send(slot(0, 1, 0), h, b_up)
        send(slot(0, -1, 0), h, b_dn)
    attention(4)
    both(slot(1, 0, -1))
    both(slot(1, 0, 1))
    send(slot(1, 0, -1), 0, b_up)
    send(slot(1, 0, 1), 1, b_dn)
    for h in range(2):
        send(slot(1, 0, 1), h, a_up)
        send(slot(1, 0, -1), h, a_dn)
    og_copy.wait()

    def slot_of(step, table, j):
        kind = 0 if j < 2 else 1
        return slot(kind, pick(step, [t[j][1] for t in table]), pick(step, [t[j][2] for t in table]))

    def tick(t):
        up, dn = slot_of(t, TICKS, 0), slot_of(t, TICKS, 1)
        up2, dn2 = slot_of(t, TICKS, 2), slot_of(t, TICKS, 3)
        for h in range(2):
            send(up, h, b_up)
            send(dn, h, b_dn)
            send(up2, h, a_up)
            send(dn2, h, a_dn)

    def last_tick():
        on_b = ((slot_of(4, TICKS, 0), b_up), (slot_of(4, TICKS, 1), b_dn))
        on_a = ((slot_of(4, TICKS, 2), a_up), (slot_of(4, TICKS, 3), a_dn))

        def go(leave, stay):
            for c in range(2):
                for r in range(2):
                    for s, peer in leave:
                        quarter_copy(s, r, c, peer).start()
                for s, peer in stay:
                    send(s, c, peer)

        @pl.when(zl == zh)
        def _():
            go(on_a, on_b)

        @pl.when(zl != zh)
        def _():
            go(on_b, on_a)

    order = []
    for step, four in enumerate(STEPS):
        here = [slot(*u) for u in four]
        if step >= 4:
            here = [jnp.where(zl == zh, here[(j + 2) % 4], here[j]) for j in range(4)]
        order.extend(here)

    def unit(step, j):
        if isinstance(step, int):
            four = order[4 * step:4 * step + 4]
            return four[j] if isinstance(j, int) else pick(j, four)
        return pick(step * 4 + j, order)

    def index_of(s):
        return (s // 16) * 8 + ((s // 4) % 2) * 4 + s % 4

    def part_of(c):
        return pl.ds(0, UNIT) if c is None else pl.ds(c * HD, HD)

    def core_copy(s, c=None):
        n = index_of(s)
        return pltpu.make_async_remote_copy(
            src_ref=part.at[s, :, part_of(c)], dst_ref=rbuf.at[n, :, part_of(c)], send_sem=csend,
            recv_sem=crecv.at[n, c or 0], device_id=c_peer, device_id_type=MESH,
        )

    def far_copy(s, c=None):
        n = index_of(s) % 8
        return pltpu.make_async_remote_copy(
            src_ref=part.at[s, :, part_of(c)], dst_ref=zbuf.at[n, :, part_of(c)], send_sem=zsend,
            recv_sem=zrecv.at[n, c or 0], device_id=far_peer, device_id_type=MESH,
        )

    def columns(n):
        return pl.ds(pl.multiple_of(n * UNIT, UNIT), UNIT)

    def hand_over(s, c=None):
        @pl.when((s // 8) % 2 != core)
        def _():
            core_copy(s, c).start()

    def add_grads(step, lo, hi):
        four = [unit(step, j) for j in range(4)]
        g = jnp.concatenate([og[:, columns(s)] for s in four], axis=1)
        for b in range(lo // UNIT, hi // UNIT):
            w = jnp.concatenate([wall[s, b * UNIT:(b + 1) * UNIT, :] for s in four], axis=1)
            acc[:, b * UNIT:(b + 1) * UNIT] += lax.dot_general(
                g, w, (((1,), (1,)), ((), ())), preferred_element_type=F32
            )

    def process(s):
        part[s] = jnp.dot(attn[...], wall[s], preferred_element_type=F32).astype(BF16)
        hand_over(s)

    def combine(s, c=None):
        @pl.when((s // 8) % 2 == core)
        def _():
            n = index_of(s)
            core_copy(s, c).wait_recv()
            p = part_of(c)
            part[s, :, p] = (part[s, :, p].astype(F32) + rbuf[n, :, p].astype(F32)).astype(BF16)

            @pl.when(s // 16 != zh)
            def _():
                far_copy(s, c).start()

    def finish_of(s, c=None):
        @pl.when(((s // 8) % 2 == core) & (s // 16 == zh))
        def _():
            n = index_of(s) % 8
            far_copy(s, c).wait_recv()
            p = part_of(c)
            at = 0 if c is None else c * HD
            wide = UNIT if c is None else HD
            out_ref[:, pl.ds(pl.multiple_of(n * UNIT + at, HD), wide)] = (
                part[s, :, p].astype(F32) + zbuf[n, :, p].astype(F32)
            ).astype(BF16)

    def finish(i, carry):
        finish_of(unit(i // 4, i % 4))
        return carry

    def step_body(step, carry):
        @pl.when(step == 1)
        def _():
            both(slot(0, 0, 1))
            both(slot(0, 0, -1))
            both(slot(0, 2, 0))
            tick(1)

        @pl.when(step == 2)
        def _():
            both(slot(1, 1, 0))
            both(slot(1, -1, 0))
            both(slot(0, 1, -1))

        @pl.when((step >= 3) & (step <= 5))
        def _():
            for j in range(4):
                both(unit(step, j))

        @pl.when((step >= 3) & (step <= 4))
        def _():
            tick(step - 1)

        @pl.when(step == 5)
        def _():
            last_tick()

        def one(j, c):
            s = unit(step, j)

            @pl.when(step == 6)
            def _():
                both(s)

            process(s)

            @pl.when(j > 0)
            def _():
                combine(unit(step, j - 1))

            return c

        lax.fori_loop(0, 4, one, 0)
        add_grads(step, 0, acc.shape[1])
        combine(unit(step, 3))

        @pl.when(step >= 2)
        def _():
            lax.fori_loop(4 * (step - 2), 4 * (step - 1), finish, 0)

        return carry

    lax.fori_loop(0, 7, step_body, 0)

    nn = (((1,), (0,)), ((), ()))
    nt = (((1,), (1,)), ((), ()))
    kg[...] = jnp.zeros_like(kg)
    vg[...] = jnp.zeros_like(vg)

    def grads(h, c):
        lanes = pl.ds(pl.multiple_of(h * HD, HD), HD)
        g32 = acc[:, lanes].astype(BF16).astype(F32)
        g = g32.astype(BF16)
        p = prob_t[lanes, :]
        weighed = (g32 * attn[:, lanes].astype(F32)).astype(BF16)
        delta = lax.dot_general(jnp.ones((8, HD), BF16), weighed, nt, preferred_element_type=F32)[0:1, :]
        gp = lax.dot_general(vall[pl.ds(0, prompt), :], g, nt, preferred_element_type=F32)
        ds = (p.astype(F32) * (gp - delta) * scale).astype(BF16)
        kg[...] += lax.dot_general(ds, qrot[:, lanes], nn, preferred_element_type=F32)
        vg[...] += lax.dot_general(p, g, nn, preferred_element_type=F32)
        return c

    def last_arrived(j, r, c):
        quarter_copy(unit(7, j), r, c, z_peer).wait_recv()

    def leaving(c):
        def one(j, carry):
            s = unit(7, j)
            if c == 0:
                last_arrived(j, 0, 0)
            last_arrived(j, 1, c)
            part[s, :, part_of(c)] = jnp.dot(
                attn[...], wall[s, :, c * HD:(c + 1) * HD], preferred_element_type=F32
            ).astype(BF16)
            hand_over(s, c)
            return carry

        lax.fori_loop(0, 2, one, 0)

    def first_half(j, c):
        s = unit(7, j)
        arrived(s, 0)
        part[s] = jnp.dot(attn[:, 0:HALF], wall[s, 0:HALF, :], preferred_element_type=F32).astype(BF16)
        return c

    def second_product(j, c):
        s = unit(7, j)
        rest = jnp.dot(attn[:, HALF:2 * HALF], wall[s, HALF:2 * HALF, :], preferred_element_type=F32)
        part[s] = (part[s].astype(F32) + rest).astype(BF16)
        hand_over(s)
        return c

    leaving(0)
    lax.fori_loop(2, 4, first_half, 0)
    combine(unit(7, 0), 0)
    combine(unit(7, 1), 0)
    lax.fori_loop(20, 24, finish, 0)
    last_arrived(0, 0, 1)
    last_arrived(1, 0, 1)
    add_grads(7, 0, HALF)
    lax.fori_loop(0, heads // 2, grads, 0, unroll=4)
    leaving(1)
    arrived(unit(7, 2), 1)
    arrived(unit(7, 3), 1)
    add_grads(7, HALF, 2 * HALF)
    combine(unit(7, 0), 1)
    combine(unit(7, 1), 1)
    lax.fori_loop(heads // 2, heads, grads, 0, unroll=4)

    n_dp = gsend.shape[0]
    own_rows = prompt // n_dp
    gsend[:, 0:own_rows, :] = kg[...].reshape(n_dp, own_rows, HD)
    gsend[:, own_rows:2 * own_rows, :] = vg[...].reshape(n_dp, own_rows, HD)

    def grad_send(j, c):
        pltpu.make_async_remote_copy(
            src_ref=gsend.at[(dp + j) % n_dp], dst_ref=grecv.at[dp], send_sem=gssem, recv_sem=grsem,
            device_id=((dp + j) % n_dp, mp), device_id_type=MESH,
        ).start()
        return c

    lax.fori_loop(1, n_dp, grad_send, 0)
    grecv[dp] = gsend[dp]
    lax.fori_loop(2, 4, second_product, 0)

    lax.fori_loop(24, 28, finish, 0)
    combine(unit(7, 2))
    combine(unit(7, 3))

    everyone = pltpu.make_async_remote_copy(
        src_ref=gsend.at[pl.ds(0, n_dp - 1)], dst_ref=grecv.at[pl.ds(0, n_dp - 1)], send_sem=gssem, recv_sem=grsem,
        device_id=z_peer, device_id_type=MESH,
    )
    everyone.wait_recv()
    total = jnp.sum(grecv[...], axis=0)
    kg_out[...] = total[0:own_rows, :]
    vg_out[...] = total[own_rows:2 * own_rows, :]
    everyone.wait_send()

    def last_finish(j, carry):
        finish_of(unit(7, j), 0)
        finish_of(unit(7, j), 1)
        return carry

    lax.fori_loop(2, 4, last_finish, 0)
    for buf, sem in ((wall.at[pl.ds(0, n_dp - 1)], wsend), (rbuf, csend), (zbuf, zsend)):
        pltpu.make_async_remote_copy(
            src_ref=buf, dst_ref=buf, send_sem=sem, recv_sem=wrecv.at[0, 0], device_id=z_peer, device_id_type=MESH
        ).wait_send()


def write_out(*refs):
    n = len(refs) // 2
    copies = [pltpu.make_async_copy(refs[i], refs[n + i], refs[2 * n].at[i]) for i in range(n)]
    for c in copies:
        c.start()
    for c in copies:
        c.wait()


def per_device(queries, keys, values, prompt_keys, prompt_values, out_weight, out_grad, lengths):
    tok, width = queries.shape
    prompt = prompt_keys.shape[0]
    n_dp = lax.axis_size("dp")
    own_rows = prompt // n_dp
    half = HD // 2
    freq = ROPE_BASE ** (-2.0 * np.arange(half) / HD)
    table = np.zeros((8, HD), np.float32)
    table[0] = np.concatenate([freq, freq])
    table[1] = np.concatenate([-np.ones(half), np.ones(half)])
    anywhere = pl.BlockSpec(memory_space=pl.ANY)
    vmem = pl.BlockSpec(memory_space=pltpu.VMEM)
    dma = pltpu.SemaphoreType.DMA
    results = pl.pallas_call(
        kernel,
        out_shape=(
            pltpu.VMEM((tok, 8 * UNIT), BF16),
            pltpu.VMEM((own_rows, HD), F32),
            pltpu.VMEM((own_rows, HD), F32),
        ),
        in_specs=[anywhere] * 7 + [pl.BlockSpec(memory_space=pltpu.SMEM), vmem],
        out_specs=(vmem, vmem, vmem),
        scratch_shapes=[
            pltpu.VMEM((n_dp, width, UNIT), BF16),
            pltpu.VMEM((tok, n_dp * UNIT), BF16),
            pltpu.VMEM((n_dp, tok, UNIT), BF16),
            pltpu.VMEM((16, tok, UNIT), BF16),
            pltpu.VMEM((8, tok, UNIT), BF16),
            pltpu.VMEM((prompt, HD), F32),
            pltpu.VMEM((prompt, HD), F32),
            pltpu.VMEM((n_dp, 2 * own_rows, HD), F32),
            pltpu.VMEM((n_dp, 2 * own_rows, HD), F32),
            pltpu.VMEM((tok, width), F32),
            pltpu.VMEM((tok, width), BF16),
            pltpu.VMEM((tok, width), BF16),
            pltpu.VMEM((width, tok), BF16),
            pltpu.VMEM((tok, width), BF16),
            pltpu.VMEM((tok, HD), BF16),
            pltpu.VMEM((prompt + tok, HD), BF16),
            pltpu.VMEM((prompt + tok, HD), BF16),
            pltpu.VMEM((tok, HD), F32),
            pltpu.VMEM((tok, HD), F32),
            pltpu.VMEM((tok, HD), jnp.int32),
            dma((7,)),
            dma,
            dma((n_dp, 4)),
            dma,
            dma((16, 2)),
            dma,
            dma((8, 2)),
            dma,
            dma,
        ],
        compiler_params=pltpu.CompilerParams(
            collective_id=0, has_side_effects=True, vmem_limit_bytes=58 * 1024 * 1024
        ),
    )(queries, keys, values, prompt_keys, prompt_values, out_weight, out_grad, lengths, jnp.asarray(table))
    return pl.pallas_call(
        write_out,
        out_shape=tuple(jax.ShapeDtypeStruct(r.shape, r.dtype) for r in results),
        in_specs=[vmem] * 3,
        out_specs=(anywhere,) * 3,
        scratch_shapes=[dma((3,))],
    )(*(pltpu.with_memory_space_constraint(r, pltpu.VMEM) for r in results))


def solution(mesh):
    in_specs = (
        P("dp", "mp"),
        P("dp", "mp"),
        P("dp", "mp"),
        P(None, "mp"),
        P(None, "mp"),
        P("mp", "dp"),
        P("dp", None),
        P("dp", None),
    )
    out_specs = (P("dp", "mp"), P("dp", "mp"), P("dp", "mp"))
    return jax.shard_map(
        per_device, mesh=mesh, in_specs=in_specs, out_specs=out_specs, check_vma=False
    )
```
